512 devices in a mesh: row: 16 (over x, z_hi), col: 32 (over z_lo, y, core).
Axes of the slice: x: 4, y: 4, z: 16 (z_hi: 4, z_lo: 4; z = z_hi * 4 + z_lo), core: 2. Of those that a mesh axis runs over, the one named last changes fastest.
Arguments:
- inverse_pool: bfloat16 [16384, 16384], P('row', 'col'), as said below
- factor_one: bfloat16 [16384, 256], P(('row', 'col')), may hold values from -0.046875 to 0.046875
- factor_two: bfloat16 [16384, 256], P(('row', 'col')), may hold values from -0.046875 to 0.046875
- diag_inv_one: float32 [256, 256], replicated, may hold values from -3 to 3
- diag_inv_two: float32 [256, 256], replicated, may hold values from -3 to 3
- struct_one: int32 [64], replicated, may hold values 0 or 1
- struct_two: int32 [64], replicated, may hold values 0 or 1
Outputs:
- column_one: bfloat16 [16384, 256], P(('row', 'col'))
- column_two: bfloat16 [16384, 256], P(('row', 'col'))
- diagonal_one: float32 [256, 256], replicated
- diagonal_two: float32 [256, 256], replicated
The draws below stay inside these ranges and needn't reach their ends.
Inputs may be any that keep to these rules, and one draw needn't show every extreme that they name: inverse_pool is symmetric: entry (i, j) equals entry (j, i).
All inputs are finite; a program needn't handle non-finite values.
Results may differ from the reference program's by a relative error of at most 0.0007.
Values may be sent and summed in bfloat16 or wider, within the bound.
No kernel may reach another device: no remote copies, remote signals or barrier semaphores. Data moves between devices by JAX's collectives and lax.ppermute only.
A program may use at most 64 MiB of HBM per device.

```python
import jax
import jax.numpy as jnp
from jax import lax

B = 256
W = 256
P_SIZE = 64
NP = 16384


def draw_inverse_pool(key, part):
    first_key = jax.random.fold_in(key, 11)
    base = jax.random.normal(first_key, (NP, NP), jnp.float32)
    whole = (base + base.T) * 0.7071
    return jnp.clip(whole, -6.0, 6.0).astype(jnp.bfloat16)


def place_ends(result, stream_key, smallest, largest):
    shape = result.shape
    spot = [jax.random.randint(jax.random.fold_in(stream_key, axis), (), 0, shape[axis]) for axis in range(len(shape))]
    result = result.at[tuple(spot)].set(smallest)
    longest = shape.index(max(shape))
    spot[longest] = (spot[longest] + 1) % shape[longest]
    return result.at[tuple(spot)].set(largest)


def block_scale(own_key, extent, split, low, top_value):
    def one(position, blocks):
        draws = jax.random.uniform(jax.random.fold_in(jax.random.fold_in(own_key, 6), position), (blocks,), jnp.float32, low / len(split), top_value / len(split))
        return jnp.repeat(jnp.exp(draws), extent[position] // blocks).reshape((-1,) + (1,) * (len(extent) - position - 1))

    loudness = one(*split[0])
    for cut in split[1:]:
        loudness = loudness * one(*cut)
    return loudness


def bell_draw(stream_key, shape, width, limit, shards=(), held_as=jnp.bfloat16):
    loudness = block_scale(stream_key, shape, shards, -0.22, 0.18) if shards else 1.0
    entries = jax.random.normal(stream_key, shape, jnp.float32) * width * loudness
    return jnp.minimum(jnp.maximum(entries, -limit), limit).astype(held_as)


def setup_inputs(seed: int = 0) -> dict:
    key_of = jax.random.split(jax.random.key(seed), 8)
    return {
        "inverse_pool": draw_inverse_pool(jax.random.fold_in(key_of[7], 71), 0),
        "factor_one": bell_draw(key_of[1], (NP, W), NP ** -0.5, 0.046875, ((0, 512),)),
        "factor_two": bell_draw(key_of[2], (NP, W), NP ** -0.5, 0.046875, ((0, 512),)),
        "diag_inv_one": bell_draw(key_of[3], (W, W), 0.5, 3.0, (), jnp.float32),
        "diag_inv_two": bell_draw(key_of[4], (W, W), 0.5, 3.0, (), jnp.float32),
        "struct_one": place_ends((jax.random.randint(key_of[5], (P_SIZE,), 0, 3) < 2).astype(jnp.int32), jax.random.fold_in(key_of[5], 1), 0, 1),
        "struct_two": place_ends((jax.random.randint(key_of[6], (P_SIZE,), 0, 3) < 2).astype(jnp.int32), jax.random.fold_in(key_of[6], 1), 0, 1),
    }


def row_mask(struct):
    return jnp.repeat(struct, B)


def reference(inverse_pool, factor_one, factor_two, diag_inv_one, diag_inv_two, struct_one, struct_two):
    mask_one = row_mask(struct_one)
    mask_two = row_mask(struct_two)
    masked_one = factor_one * mask_one.astype(jnp.bfloat16)[:, None]
    masked_two = factor_two * mask_two.astype(jnp.bfloat16)[:, None]
    stacked = jnp.concatenate([masked_one, masked_two], axis=1)
    blocks = inverse_pool.reshape(P_SIZE, B, NP)
    product = lax.map(lambda slab: jnp.dot(slab, stacked, preferred_element_type=jnp.float32), blocks)
    product = product.reshape(NP, 2 * W)
    product_one = product[:, :W]
    product_two = product[:, W:]
    column_one = (-(product_one * mask_one.astype(jnp.float32)[:, None])).astype(jnp.bfloat16)
    column_two = (-(product_two * mask_two.astype(jnp.float32)[:, None])).astype(jnp.bfloat16)
    diagonal_one = diag_inv_one + jnp.dot(masked_one.astype(jnp.float32).T, product_one, precision=lax.Precision.HIGHEST, preferred_element_type=jnp.float32)
    diagonal_two = diag_inv_two + jnp.dot(masked_two.astype(jnp.float32).T, product_two, precision=lax.Precision.HIGHEST, preferred_element_type=jnp.float32)
    return column_one, column_two, diagonal_one, diagonal_two
```

```python
import jax
import jax.numpy as jnp
from jax import lax
from jax.sharding import Mesh, PartitionSpec as P

B = 256
AXES = ("x", "zh", "zl", "y", "core")
SIZES = (4, 4, 4, 4, 2)
ROWS = 16
COLS = 32


def exchange(parts, axes):
    return lax.all_to_all(parts, axes, 0, 0)


def gather(block, axes, count):
    return exchange(jnp.broadcast_to(block[None], (count, *block.shape)), axes)


def per_device(
    inverse_pool, factor_one, factor_two, diag_inv_one, diag_inv_two, struct_one, struct_two
):
    row_count, width = factor_one.shape
    half = width // 2
    row = lax.axis_index(("x", "zh"))
    col = lax.axis_index(("zl", "y", "core"))
    own_block = (row * COLS + col) * row_count // B
    there_block = (col * ROWS + row) * row_count // B
    masked = jnp.concatenate(
        [
            factor_one * struct_one[own_block].astype(jnp.bfloat16),
            factor_two * struct_two[own_block].astype(jnp.bfloat16),
        ],
        axis=1,
    )
    swap = [(c * ROWS + r, r * COLS + c) for r in range(ROWS) for c in range(COLS)]
    masked_there = lax.ppermute(masked, AXES, swap)

    pair = gather(masked, "core", 2).reshape(2 * row_count, 2 * width)
    strip = gather(pair, ("zl", "y"), 16).reshape(-1, 2 * width)
    partial = lax.dot_general(
        inverse_pool, strip, (((0,), (0,)), ((), ())), preferred_element_type=jnp.float32
    )
    product = jnp.sum(exchange(partial.reshape(4, -1, 2 * width), "x"), axis=0)
    product = jnp.sum(exchange(product.reshape(4, -1, 2 * width), "zh"), axis=0)
    product_one = product[:, :width]
    product_two = product[:, width:]

    mask_one = struct_one[there_block].astype(jnp.float32)
    mask_two = struct_two[there_block].astype(jnp.float32)
    column = jnp.concatenate([-(product_one * mask_one), -(product_two * mask_two)], axis=1)
    column = lax.ppermute(column.astype(jnp.bfloat16), AXES, [(b, a) for a, b in swap])

    def blocks(left, right):
        term = lax.dot_general(
            left.astype(jnp.float32),
            right,
            (((0,), (0,)), ((), ())),
            precision=lax.Precision.HIGHEST,
            preferred_element_type=jnp.float32,
        )
        return [term[:half, :half], term[:half, half:], term[half:, half:]]

    packed = jnp.concatenate(
        blocks(masked_there[:, :width], product_one) + blocks(masked_there[:, width:], product_two),
        axis=0,
    )
    shard = jnp.sum(exchange(packed.reshape(32, -1, half), ("x", "y", "core")), axis=0)
    shard = jnp.sum(gather(shard, ("zh", "zl"), 16), axis=0)
    total = gather(shard, ("x", "y", "core"), 32).reshape(2, 3, half, half)

    def whole(t):
        return jnp.concatenate(
            [
                jnp.concatenate([t[0], t[1]], axis=1),
                jnp.concatenate([t[1].T, t[2]], axis=1),
            ],
            axis=0,
        )

    return (
        column[:, :width],
        column[:, width:],
        diag_inv_one + whole(total[0]),
        diag_inv_two + whole(total[1]),
    )


def solution(mesh):
    fine = Mesh(mesh.devices.reshape(SIZES), AXES)
    rows = P(AXES, None)
    in_specs = (P(("x", "zh"), ("zl", "y", "core")), rows, rows, P(), P(), P(), P())
    out_specs = (rows, rows, P(), P())
    return jax.shard_map(
        per_device, mesh=fine, in_specs=in_specs, out_specs=out_specs, check_vma=False
    )
```

```python
import jax
import jax.numpy as jnp
from jax import lax
from jax.sharding import Mesh, PartitionSpec as P

B = 256
AXES = ("x", "zh", "zl", "y", "core")
SIZES = (4, 4, 4, 4, 2)
SWAP = [(0, 1), (1, 0)]


def exchange(parts, axes):
    return lax.all_to_all(parts, axes, 0, 0)


def gather(block, axes, count):
    return exchange(jnp.broadcast_to(block[None], (count, *block.shape)), axes)


def device_id(chip_row, chip_col, core):
    return (chip_row * 16 + chip_col) * 2 + core


def home_chip(chip_row, core):
    x, zh = chip_row // 4, chip_row % 4
    return ((x >> 1) ^ core) * 8 + (x & 1) * 4 + zh


def per_device(
    inverse_pool, factor_one, factor_two, diag_inv_one, diag_inv_two, struct_one, struct_two
):
    row_count, width = factor_one.shape
    half = width // 2
    x = lax.axis_index("x")
    chip_row = lax.axis_index(("x", "zh"))
    chip_col = lax.axis_index(("zl", "y"))
    core = lax.axis_index("core")
    first = core == 0
    struct = jnp.where(first, struct_one, struct_two)
    mask_here = struct[chip_row * 4 + lax.axis_index("zl")]
    mask_there = struct[chip_col * 4 + ((x >> 1) ^ core) * 2 + (x & 1)]

    sibling_pool = lax.ppermute(inverse_pool, "core", SWAP)
    rows = exchange(jnp.stack([factor_one, factor_two]), "core").reshape(2 * row_count, width)
    rows = rows * mask_here.astype(jnp.bfloat16)
    there = [
        (device_id(chip, home_chip(chip_r, k), k), device_id(chip_r, chip, k))
        for chip_r in range(16)
        for chip in range(16)
        for k in range(2)
    ]
    rows_there = lax.ppermute(rows, AXES, there)
    strip = gather(rows, ("zl", "y"), 16).reshape(-1, width)

    partial = lax.dot_general(
        jnp.concatenate([inverse_pool, sibling_pool], axis=1),
        strip,
        (((0,), (0,)), ((), ())),
        preferred_element_type=jnp.float32,
    )
    product = jnp.sum(exchange(partial.reshape(4, -1, width), "x"), axis=0)
    product = jnp.sum(exchange(product.reshape(4, -1, width), "zh"), axis=0)

    column = (-(product * mask_there.astype(jnp.float32))).astype(jnp.bfloat16)
    column = column.reshape(2, row_count, width)
    back = [(b, a) for a, b in there]
    cross = [(b, a ^ 1) for a, b in there]
    mine = lax.ppermute(jnp.where(first, column[0], column[1]), AXES, back)
    other = lax.ppermute(jnp.where(first, column[1], column[0]), AXES, cross)

    def term(left, right):
        return lax.dot_general(
            rows_there[:, left].astype(jnp.float32),
            product[:, right],
            (((0,), (0,)), ((), ())),
            precision=lax.Precision.HIGHEST,
            preferred_element_type=jnp.float32,
        )

    low, high = slice(0, half), slice(half, width)
    packed = jnp.concatenate([term(low, low), term(low, high), term(high, high)], axis=0)
    shard = jnp.sum(exchange(packed.reshape(16, -1, half), ("x", "y")), axis=0)
    shard = jnp.sum(gather(shard, ("zh", "zl"), 16), axis=0)
    total = gather(shard, ("x", "y"), 16).reshape(3, half, half)
    sibling = lax.ppermute(total, "core", SWAP)

    def whole(t):
        return jnp.concatenate(
            [
                jnp.concatenate([t[0], t[1]], axis=1),
                jnp.concatenate([t[1].T, t[2]], axis=1),
            ],
            axis=0,
        )

    return (
        jnp.where(first, mine, other),
        jnp.where(first, other, mine),
        diag_inv_one + whole(jnp.where(first, total, sibling)),
        diag_inv_two + whole(jnp.where(first, sibling, total)),
    )


def solution(mesh):
    fine = Mesh(mesh.devices.reshape(SIZES), AXES)
    rows = P(AXES, None)
    in_specs = (P(("x", "zh"), ("zl", "y", "core")), rows, rows, P(), P(), P(), P())
    out_specs = (rows, rows, P(), P())
    return jax.shard_map(
        per_device, mesh=fine, in_specs=in_specs, out_specs=out_specs, check_vma=False
    )
```

```python
import jax
import jax.numpy as jnp
from jax import lax
from jax.sharding import Mesh, PartitionSpec as P

AXES = ("x", "zh", "zl", "y", "core")
SIZES = (4, 4, 4, 4, 2)
SWAP = [(0, 1), (1, 0)]


def exchange(parts, axes):
    return lax.all_to_all(parts, axes, 0, 0)


def gather(block, axes, count):
    return exchange(jnp.broadcast_to(block[None], (count, *block.shape)), axes)


def device_id(x, zh, zl, y, core):
    return (((x * 4 + zh) * 4 + zl) * 4 + y) * 2 + core


TURN = [
    (device_id(a, b, c, d, k), device_id(d, c, a, b, k))
    for a in range(4)
    for b in range(4)
    for c in range(4)
    for d in range(4)
    for k in range(2)
]


def per_device(
    inverse_pool, factor_one, factor_two, diag_inv_one, diag_inv_two, struct_one, struct_two
):
    row_count, width = factor_one.shape
    half = width // 2
    chunk = 2 * row_count
    core = lax.axis_index("core")
    first = core == 0
    struct = jnp.where(first, struct_one, struct_two)
    mask = lax.dynamic_slice_in_dim(struct, lax.axis_index(("x", "zh")) * 4, 4)

    pool = inverse_pool.reshape(4, 4, chunk, -1).transpose(1, 0, 2, 3).reshape(inverse_pool.shape)
    sibling_pool = lax.ppermute(pool, "core", SWAP)

    both = jnp.broadcast_to(
        jnp.stack([factor_one, factor_two])[None], (4, 2, row_count, width)
    ).reshape(8, row_count, width)
    rows = exchange(both, ("zl", "core")).reshape(4, chunk, width)
    rows = rows * mask.astype(jnp.bfloat16)[:, None, None]
    strip = gather(lax.ppermute(rows, AXES, TURN), "x", 4)

    def part(which):
        piece = lax.dynamic_slice_in_dim(strip, 2 * which, 2, axis=1)
        return piece.transpose(1, 0, 2, 3).reshape(-1, width)

    partial = jnp.dot(pool, part(core), preferred_element_type=jnp.float32) + jnp.dot(
        sibling_pool, part(1 - core), preferred_element_type=jnp.float32
    )
    product = jnp.sum(exchange(partial.reshape(4, -1, width), "y"), axis=0)

    column = jnp.sum(exchange(product.reshape(4, chunk, width), "zl"), axis=0)
    own = lax.dynamic_index_in_dim(mask, lax.axis_index("zl"), keepdims=False)
    column = (-(column * own.astype(jnp.float32))).astype(jnp.bfloat16)
    column = exchange(column.reshape(2, row_count, width), "core")

    flat = rows.reshape(-1, width).astype(jnp.float32)

    def term(left, right):
        return lax.dot_general(
            flat[:, left],
            product[:, right],
            (((0,), (0,)), ((), ())),
            precision=lax.Precision.HIGHEST,
            preferred_element_type=jnp.float32,
        )

    low, high = slice(0, half), slice(half, width)
    packed = jnp.concatenate([term(low, low), term(low, high), term(high, high)], axis=0)
    shard = jnp.sum(exchange(packed.reshape(16, -1, half), ("x", "y")), axis=0)
    shard = jnp.sum(gather(shard, ("zh", "zl"), 16), axis=0)
    total = gather(shard, ("x", "y"), 16).reshape(3, half, half)
    sibling = lax.ppermute(total, "core", SWAP)

    def whole(t):
        return jnp.concatenate(
            [
                jnp.concatenate([t[0], t[1]], axis=1),
                jnp.concatenate([t[1].T, t[2]], axis=1),
            ],
            axis=0,
        )

    return (
        column[0],
        column[1],
        diag_inv_one + whole(jnp.where(first, total, sibling)),
        diag_inv_two + whole(jnp.where(first, sibling, total)),
    )


def solution(mesh):
    fine = Mesh(mesh.devices.reshape(SIZES), AXES)
    rows = P(AXES, None)
    in_specs = (P(("x", "zh"), ("zl", "y", "core")), rows, rows, P(), P(), P(), P())
    out_specs = (rows, rows, P(), P())
    return jax.shard_map(
        per_device, mesh=fine, in_specs=in_specs, out_specs=out_specs, check_vma=False
    )
```

```python
import jax
import jax.numpy as jnp
from jax import lax
from jax.experimental import pallas as pl
from jax.experimental.pallas import tpu as pltpu
from jax.sharding import Mesh, PartitionSpec as P

AXES = ("x", "zh", "zl", "y", "core")
SIZES = (4, 4, 4, 4, 2)
SWAP = [(0, 1), (1, 0)]
VMEM = pl.BlockSpec(memory_space=pltpu.VMEM)
SMEM = pl.BlockSpec(memory_space=pltpu.SMEM)
PARAMS = pltpu.CompilerParams(vmem_limit_bytes=32 * 1024 * 1024)


def exchange(parts, axes):
    return lax.all_to_all(parts, axes, 0, 0)


def gather(block, axes, count):
    return exchange(jnp.broadcast_to(block[None], (count, *block.shape)), axes)


def device_id(x, zh, zl, y, core):
    return (((x * 4 + zh) * 4 + zl) * 4 + y) * 2 + core


def turn_source(x, zh, zl, y):
    near = (1, 2, 3, 0) if zl < 2 else (2, 3, 0, 1)
    return zl, y, near[(zh - y) % 4], (y + 2 + x - zl) % 4


TURN = [
    (device_id(*turn_source(a, b, c, d), k), device_id(a, b, c, d, k))
    for a in range(4)
    for b in range(4)
    for c in range(4)
    for d in range(4)
    for k in range(2)
]


def multiply_kernel(pool, sibling, strip, out, rhs):
    core = lax.axis_index("core")
    shift = lax.axis_index("zl") - lax.axis_index("y") + 2
    depth = rhs.shape[0] // 2
    for side, which in ((0, core), (1, 1 - core)):
        for h in range(2):
            for j in range(4):
                start = side * depth + h * 256 + j * 64
                rhs[start : start + 64] = strip[(j + shift) & 3, 2 * which + h]
    for z in range(4):
        rows = slice(z * 256, (z + 1) * 256)
        block = jnp.dot(
            pool[rows], rhs[:depth], preferred_element_type=jnp.float32
        ) + jnp.dot(sibling[rows], rhs[depth:], preferred_element_type=jnp.float32)
        for y in range(4):
            out[y, z] = block[y * 64 : (y + 1) * 64]


def diagonal_kernel(parts, rows, packed, pieces):
    product = parts[0] + parts[1] + parts[2] + parts[3]
    left = rows[...]
    term = jnp.zeros((256, 256), jnp.float32)
    rest = product
    for _ in range(3):
        piece = rest.astype(jnp.bfloat16)
        rest = rest - piece.astype(jnp.float32)
        term = term + lax.dot_general(
            left, piece, (((0,), (0,)), ((), ())), preferred_element_type=jnp.float32
        )
    packed[0:128] = term[:128, :128]
    packed[128:256] = term[:128, 128:]
    packed[256:384] = term[128:, 128:]
    for z in range(4):
        pieces[z, 0:64] = product[z * 64 : (z + 1) * 64, :128]
        pieces[z, 64:128] = product[z * 64 : (z + 1) * 64, 128:]


def join_kernel(parts, pieces, out):
    shard = parts[0]
    for i in range(1, 16):
        shard = shard + parts[i]
    for z in range(4):
        out[z, 0:128] = pieces[z]
        out[z, 128:152] = shard


def split_kernel(mask, parts, shards, stay, leave):
    core = lax.axis_index("core")
    own = -mask[lax.axis_index("zl")].astype(jnp.float32)
    summed = parts[0] + parts[1] + parts[2] + parts[3]
    for i in range(4):
        shards[i] = summed[128:152]
    column = summed[0:128] * own
    low = jnp.concatenate([column[0:32], column[64:96]])
    high = jnp.concatenate([column[32:64], column[96:128]])
    stay[...] = jnp.where(core == 0, low, high)
    leave[...] = jnp.where(core == 0, high, low)


def finish_kernel(mine, swapped, inv_one, inv_two, column_one, column_two, diag_one, diag_two):
    first = lax.axis_index("core") == 0
    own, other = mine[...], swapped[...]
    one = jnp.where(first, own, other)
    two = jnp.where(first, other, own)
    for t, inv, diag, column in (
        (one, inv_one, diag_one, column_one),
        (two, inv_two, diag_two, column_two),
    ):
        diag[0:128, 0:128] = inv[0:128, 0:128] + t[0:128]
        diag[0:128, 128:256] = inv[0:128, 128:256] + t[128:256]
        diag[128:256, 0:128] = inv[128:256, 0:128] + t[128:256].T
        diag[128:256, 128:256] = inv[128:256, 128:256] + t[256:384]
        column[:, 0:128] = t[384:416].astype(jnp.bfloat16)
        column[:, 128:256] = t[416:448].astype(jnp.bfloat16)


def call(kernel, outs, args, scratch=(), scalars=0):
    many = isinstance(outs, list)
    return pl.pallas_call(
        kernel,
        out_shape=outs,
        in_specs=[SMEM] * scalars + [VMEM] * (len(args) - scalars),
        out_specs=[VMEM] * len(outs) if many else VMEM,
        scratch_shapes=list(scratch),
        compiler_params=PARAMS,
    )(*args)


def per_device(
    inverse_pool, factor_one, factor_two, diag_inv_one, diag_inv_two, struct_one, struct_two
):
    row_count, width = factor_one.shape
    f32 = jnp.float32
    core = lax.axis_index("core")
    first = core == 0
    struct = jnp.where(first, struct_one, struct_two)
    mask = lax.dynamic_slice_in_dim(struct, lax.axis_index(("x", "zh")) * 4, 4)
    sibling_pool = lax.ppermute(inverse_pool, "core", SWAP)

    both = jnp.broadcast_to(
        jnp.stack([factor_one, factor_two])[None], (4, 2, row_count, width)
    ).reshape(8, row_count, width)
    rows = exchange(both, ("zl", "core")).reshape(4, 2 * row_count, width)
    rows = rows * mask.astype(jnp.bfloat16)[:, None, None]
    rows = lax.optimization_barrier(rows)
    strip = gather(lax.ppermute(rows, AXES, TURN), "x", 4)

    partial = call(
        multiply_kernel,
        jax.ShapeDtypeStruct((4, 4, 64, 256), f32),
        (inverse_pool, sibling_pool, strip),
        [pltpu.VMEM((1024, 256), jnp.bfloat16)],
    )
    parts = exchange(partial.reshape(4, 256, width), "y")
    packed, pieces = call(
        diagonal_kernel,
        [jax.ShapeDtypeStruct((384, 128), f32), jax.ShapeDtypeStruct((4, 128, 128), f32)],
        (parts, rows.reshape(256, width)),
    )
    parts = exchange(packed.reshape(16, 24, 128), ("x", "y"))
    joined = call(join_kernel, jax.ShapeDtypeStruct((4, 152, 128), f32), (parts, pieces))
    quarter = jax.ShapeDtypeStruct((2 * row_count, 128), f32)
    shards, stay, leave = call(
        split_kernel,
        [jax.ShapeDtypeStruct((4, 24, 128), f32), quarter, quarter],
        (mask, exchange(joined, "zl")),
        scalars=1,
    )
    shard = jnp.sum(exchange(shards, "zh"), axis=0)
    total = gather(shard, ("x", "y"), 16).reshape(384, 128)
    swapped = lax.ppermute(jnp.concatenate([total, leave]), "core", SWAP)
    wide = jax.ShapeDtypeStruct((row_count, width), jnp.bfloat16)
    square = jax.ShapeDtypeStruct((width, width), f32)
    return tuple(
        call(
            finish_kernel,
            [wide, wide, square, square],
            (jnp.concatenate([total, stay]), swapped, diag_inv_one, diag_inv_two),
        )
    )


def solution(mesh):
    fine = Mesh(mesh.devices.reshape(SIZES), AXES)
    rows = P(AXES, None)
    in_specs = (P(("x", "zh"), ("zl", "y", "core")), rows, rows, P(), P(), P(), P())
    out_specs = (rows, rows, P(), P())
    return jax.shard_map(
        per_device, mesh=fine, in_specs=in_specs, out_specs=out_specs, check_vma=False
    )
```

```python
import jax
import jax.numpy as jnp
from jax import lax
from jax.experimental import pallas as pl
from jax.experimental.pallas import tpu as pltpu
from jax.sharding import Mesh, PartitionSpec as P

AXES = ("x", "zh", "zl", "y", "core")
SIZES = (4, 4, 4, 4, 2)
SWAP = [(0, 1), (1, 0)]
VMEM = pl.BlockSpec(memory_space=pltpu.VMEM)
SMEM = pl.BlockSpec(memory_space=pltpu.SMEM)
PARAMS = pltpu.CompilerParams(vmem_limit_bytes=32 * 1024 * 1024)


def exchange(parts, axes):
    return lax.all_to_all(parts, axes, 0, 0)


def gather(block, axes, count):
    return exchange(jnp.broadcast_to(block[None], (count, *block.shape)), axes)


def rotate(parts, axis):
    return [parts[0]] + [
        lax.ppermute(parts[s], axis, [(i, (i + s) % 4) for i in range(4)]) for s in (1, 2, 3)
    ]


def device_id(x, zh, zl, y, core):
    return (((x * 4 + zh) * 4 + zl) * 4 + y) * 2 + core


def turn_source(x, zh, zl, y):
    near = (1, 2, 3, 0) if zl < 2 else (2, 3, 0, 1)
    return zl, y, near[(zh - y) % 4], (y + 2 + x - zl) % 4


TURN = [
    (device_id(*turn_source(a, b, c, d), k), device_id(a, b, c, d, k))
    for a in range(4)
    for b in range(4)
    for c in range(4)
    for d in range(4)
    for k in range(2)
]


def multiply_kernel(pool, sibling, strip, rows, diag, out0, out1, out2, out3, rhs, full):
    core, y = lax.axis_index("core"), lax.axis_index("y")
    shift = lax.axis_index("zl") - y + 2
    depth = rhs.shape[0] // 2
    for side, which in ((0, core), (1, 1 - core)):
        for h in range(2):
            for j in range(4):
                start = side * depth + h * 256 + j * 64
                rhs[start : start + 64] = strip[(j + shift) & 3, 2 * which + h]
    for z in range(4):
        take = slice(z * 256, (z + 1) * 256)
        block = jnp.dot(
            pool[take], rhs[:depth], preferred_element_type=jnp.float32
        ) + jnp.dot(sibling[take], rhs[depth:], preferred_element_type=jnp.float32)
        for j in range(4):
            full[j, z * 64 : (z + 1) * 64] = block[j * 64 : (j + 1) * 64]
    term = jnp.zeros((256, 256), jnp.float32)
    for j in range(4):
        left, rest = rows[j], full[j]
        for _ in range(3):
            piece = rest.astype(jnp.bfloat16)
            rest = rest - piece.astype(jnp.float32)
            term = term + lax.dot_general(
                left, piece, (((0,), (0,)), ((), ())), preferred_element_type=jnp.float32
            )
    diag[0:256] = term[:, :128]
    diag[256:512] = term[:, 128:]
    for hop, out in enumerate((out0, out1, out2, out3)):
        out[...] = full[(y + hop) & 3]


def turn_kernel(in0, in1, in2, in3, out0, out1, out2, out3, full):
    zl = lax.axis_index("zl")
    full[...] = in0[...] + in1[...] + in2[...] + in3[...]
    for hop, out in enumerate((out0, out1, out2, out3)):
        out[...] = full[pl.ds(pl.multiple_of(((zl + hop) & 3) * 64, 64), 64)]


def split_kernel(mask, in0, in1, in2, in3, stay, leave):
    core = lax.axis_index("core")
    own = -mask[lax.axis_index("zl")].astype(jnp.float32)
    column = (in0[...] + in1[...] + in2[...] + in3[...]) * own
    low = jnp.concatenate([column[0:32, 0:128], column[0:32, 128:256]])
    high = jnp.concatenate([column[32:64, 0:128], column[32:64, 128:256]])
    stay[...] = jnp.where(core == 0, low, high)
    leave[...] = jnp.where(core == 0, high, low)


def finish_kernel(total, stay, swapped, inv_one, inv_two, column_one, column_two, diag_one, diag_two):
    first = lax.axis_index("core") == 0
    own, other = total[...], swapped[0:512]
    own_column, other_column = stay[...], swapped[512:576]
    for swap, inv, diag, column in (
        (False, inv_one, diag_one, column_one),
        (True, inv_two, diag_two, column_two),
    ):
        pick = first != swap
        t = jnp.where(pick, own, other)
        c = jnp.where(pick, own_column, other_column).astype(jnp.bfloat16)
        diag[:, 0:128] = inv[:, 0:128] + t[0:256]
        diag[:, 128:256] = inv[:, 128:256] + t[256:512]
        column[:, 0:128] = c[0:32]
        column[:, 128:256] = c[32:64]


def call(kernel, outs, args, scratch=(), scalars=0):
    many = isinstance(outs, list)
    return pl.pallas_call(
        kernel,
        out_shape=outs,
        in_specs=[SMEM] * scalars + [VMEM] * (len(args) - scalars),
        out_specs=[VMEM] * len(outs) if many else VMEM,
        scratch_shapes=list(scratch),
        compiler_params=PARAMS,
    )(*args)


def per_device(
    inverse_pool, factor_one, factor_two, diag_inv_one, diag_inv_two, struct_one, struct_two
):
    row_count, width = factor_one.shape
    f32 = jnp.float32
    core = lax.axis_index("core")
    first = core == 0
    struct = jnp.where(first, struct_one, struct_two)
    mask = lax.dynamic_slice_in_dim(struct, lax.axis_index(("x", "zh")) * 4, 4)
    sibling_pool = lax.ppermute(inverse_pool, "core", SWAP)

    both = jnp.broadcast_to(
        jnp.stack([factor_one, factor_two])[None], (4, 2, row_count, width)
    ).reshape(8, row_count, width)
    rows = exchange(both, ("zl", "core")).reshape(4, 2 * row_count, width)
    rows = rows * mask.astype(jnp.bfloat16)[:, None, None]
    rows = lax.optimization_barrier(rows)
    strip = gather(lax.ppermute(rows, AXES, TURN), "x", 4)
    around = gather(rows, "y", 4).reshape(4, 256, width)

    quarter = jax.ShapeDtypeStruct((256, width), f32)
    diag, *parts = call(
        multiply_kernel,
        [jax.ShapeDtypeStruct((512, 128), f32)] + [quarter] * 4,
        (inverse_pool, sibling_pool, strip, around),
        [pltpu.VMEM((1024, width), jnp.bfloat16), pltpu.VMEM((4, 256, width), f32)],
    )
    shard = jnp.sum(exchange(diag.reshape(64, 8, 128), ("x", "y", "zl")), axis=0)
    parts = rotate(parts, "y")
    shard = jnp.sum(gather(shard, ("zh", "zl"), 16).reshape(4, 32, 128), axis=0)
    parts = call(
        turn_kernel,
        [jax.ShapeDtypeStruct((2 * row_count, width), f32)] * 4,
        parts,
        [pltpu.VMEM((256, width), f32)],
    )
    parts = rotate(parts, "zl")
    half = jax.ShapeDtypeStruct((2 * row_count, 128), f32)
    stay, leave = call(split_kernel, [half, half], (mask, *parts), scalars=1)
    total = gather(shard, ("x", "y"), 16).reshape(512, 128)
    swapped = lax.ppermute(jnp.concatenate([total, leave]), "core", SWAP)
    wide = jax.ShapeDtypeStruct((row_count, width), jnp.bfloat16)
    square = jax.ShapeDtypeStruct((width, width), f32)
    return tuple(
        call(
            finish_kernel,
            [wide, wide, square, square],
            (total, stay, swapped, diag_inv_one, diag_inv_two),
        )
    )


def solution(mesh):
    fine = Mesh(mesh.devices.reshape(SIZES), AXES)
    rows = P(AXES, None)
    in_specs = (P(("x", "zh"), ("zl", "y", "core")), rows, rows, P(), P(), P(), P())
    out_specs = (rows, rows, P(), P())
    return jax.shard_map(
        per_device, mesh=fine, in_specs=in_specs, out_specs=out_specs, check_vma=False
    )
```

```python
import jax
import jax.numpy as jnp
from jax import lax
from jax.experimental import pallas as pl
from jax.experimental.pallas import tpu as pltpu
from jax.sharding import Mesh, PartitionSpec as P

AXES = ("x", "zh", "zl", "y", "core")
SIZES = (4, 4, 4, 4, 2)
SWAP = [(0, 1), (1, 0)]
VMEM = pl.BlockSpec(memory_space=pltpu.VMEM)
SMEM = pl.BlockSpec(memory_space=pltpu.SMEM)
PARAMS = pltpu.CompilerParams(vmem_limit_bytes=32 * 1024 * 1024)


def exchange(parts, axes):
    return lax.all_to_all(parts, axes, 0, 0)


def gather(block, axes, count):
    return exchange(jnp.broadcast_to(block[None], (count, *block.shape)), axes)


def rotate(parts, axis):
    return [parts[0]] + [
        lax.ppermute(parts[s], axis, [(i, (i + s) % 4) for i in range(4)]) for s in (1, 2, 3)
    ]


def device_id(x, zh, zl, y, core):
    return (((x * 4 + zh) * 4 + zl) * 4 + y) * 2 + core


def turn_source(x, zh, zl, y):
    near = (1, 2, 3, 0) if zl < 2 else (2, 3, 0, 1)
    return zl, y, near[(zh - y) % 4], (y + 2 + x - zl) % 4


TURN = [
    (device_id(*turn_source(a, b, c, d), k), device_id(a, b, c, d, k))
    for a in range(4)
    for b in range(4)
    for c in range(4)
    for d in range(4)
    for k in range(2)
]


def multiply_kernel(pool, sibling, strip, rows, diag, out0, out1, out2, out3, rhs, full):
    core, y = lax.axis_index("core"), lax.axis_index("y")
    shift = lax.axis_index("zl") - y + 2
    depth = rhs.shape[0] // 2
    for side, which in ((0, core), (1, 1 - core)):
        for h in range(2):
            for j in range(4):
                start = side * depth + h * 256 + j * 64
                rhs[start : start + 64] = strip[(j + shift) & 3, 2 * which + h]
    for z in range(4):
        take = slice(z * 256, (z + 1) * 256)
        block = jnp.dot(
            pool[take], rhs[:depth], preferred_element_type=jnp.float32
        ) + jnp.dot(sibling[take], rhs[depth:], preferred_element_type=jnp.float32)
        for j in range(4):
            full[j, z * 64 : (z + 1) * 64] = block[j * 64 : (j + 1) * 64]
    term = jnp.zeros((256, 256), jnp.float32)
    for j in range(4):
        left, rest = rows[j].T, full[j]
        for _ in range(3):
            piece = rest.astype(jnp.bfloat16)
            rest = rest - piece.astype(jnp.float32)
            term = term + jnp.dot(left, piece, preferred_element_type=jnp.float32)
    diag[0:256] = term[:, :128]
    diag[256:512] = term[:, 128:]
    for hop, out in enumerate((out0, out1, out2, out3)):
        out[...] = full[(y + hop) & 3]


def turn_kernel(in0, in1, in2, in3, out0, out1, out2, out3, full):
    zl = lax.axis_index("zl")
    full[...] = in0[...] + in1[...] + in2[...] + in3[...]
    for hop, out in enumerate((out0, out1, out2, out3)):
        out[...] = full[pl.ds(pl.multiple_of(((zl + hop) & 3) * 64, 64), 64)]


def split_kernel(mask, in0, in1, in2, in3, stay, leave):
    core = lax.axis_index("core")
    own = -mask[lax.axis_index("zl")].astype(jnp.float32)
    column = (in0[...] + in1[...] + in2[...] + in3[...]) * own
    low = jnp.concatenate([column[0:32, 0:128], column[0:32, 128:256]])
    high = jnp.concatenate([column[32:64, 0:128], column[32:64, 128:256]])
    stay[...] = jnp.where(core == 0, low, high)
    leave[...] = jnp.where(core == 0, high, low)


def finish_kernel(total, stay, swapped, inv_one, inv_two, column_one, column_two, diag_one, diag_two):
    first = lax.axis_index("core") == 0
    own, other = total[...], swapped[0:512]
    own_column, other_column = stay[...], swapped[512:576]
    for swap, inv, diag, column in (
        (False, inv_one, diag_one, column_one),
        (True, inv_two, diag_two, column_two),
    ):
        pick = first != swap
        t = jnp.where(pick, own, other)
        c = jnp.where(pick, own_column, other_column).astype(jnp.bfloat16)
        diag[:, 0:128] = inv[:, 0:128] + t[0:256]
        diag[:, 128:256] = inv[:, 128:256] + t[256:512]
        column[:, 0:128] = c[0:32]
        column[:, 128:256] = c[32:64]


def call(kernel, outs, args, scratch=(), scalars=0):
    many = isinstance(outs, list)
    return pl.pallas_call(
        kernel,
        out_shape=outs,
        in_specs=[SMEM] * scalars + [VMEM] * (len(args) - scalars),
        out_specs=[VMEM] * len(outs) if many else VMEM,
        scratch_shapes=list(scratch),
        compiler_params=PARAMS,
    )(*args)


def per_device(
    inverse_pool, factor_one, factor_two, diag_inv_one, diag_inv_two, struct_one, struct_two
):
    row_count, width = factor_one.shape
    f32 = jnp.float32
    core = lax.axis_index("core")
    first = core == 0
    struct = jnp.where(first, struct_one, struct_two)
    mask = lax.dynamic_slice_in_dim(struct, lax.axis_index(("x", "zh")) * 4, 4)
    sibling_pool = lax.ppermute(inverse_pool, "core", SWAP)

    both = jnp.broadcast_to(
        jnp.stack([factor_one, factor_two])[None], (4, 2, row_count, width)
    ).reshape(8, row_count, width)
    rows = exchange(both, ("zl", "core")).reshape(4, 2 * row_count, width)
    rows = rows * mask.astype(jnp.bfloat16)[:, None, None]
    rows = lax.optimization_barrier(rows)
    strip = gather(lax.ppermute(rows, AXES, TURN), "x", 4)
    around = gather(rows, "y", 4).reshape(4, 256, width)

    quarter = jax.ShapeDtypeStruct((256, width), f32)
    diag, *parts = call(
        multiply_kernel,
        [jax.ShapeDtypeStruct((512, 128), f32)] + [quarter] * 4,
        (inverse_pool, sibling_pool, strip, around),
        [pltpu.VMEM((1024, width), jnp.bfloat16), pltpu.VMEM((4, 256, width), f32)],
    )
    shard = jnp.sum(exchange(diag.reshape(64, 8, 128), ("x", "y", "zl")), axis=0)
    parts = rotate(parts, "y")
    shard, parts = lax.optimization_barrier((shard, parts))
    shard = jnp.sum(gather(shard, ("zh", "zl"), 16).reshape(4, 32, 128), axis=0)
    parts = call(
        turn_kernel,
        [jax.ShapeDtypeStruct((2 * row_count, width), f32)] * 4,
        parts,
        [pltpu.VMEM((256, width), f32)],
    )
    parts = rotate(parts, "zl")
    shard, parts = lax.optimization_barrier((shard, parts))
    half = jax.ShapeDtypeStruct((2 * row_count, 128), f32)
    stay, leave = call(split_kernel, [half, half], (mask, *parts), scalars=1)
    total = gather(shard, ("x", "y"), 16).reshape(512, 128)
    swapped = lax.ppermute(jnp.concatenate([total, leave]), "core", SWAP)
    wide = jax.ShapeDtypeStruct((row_count, width), jnp.bfloat16)
    square = jax.ShapeDtypeStruct((width, width), f32)
    return tuple(
        call(
            finish_kernel,
            [wide, wide, square, square],
            (total, stay, swapped, diag_inv_one, diag_inv_two),
        )
    )


def solution(mesh):
    fine = Mesh(mesh.devices.reshape(SIZES), AXES)
    rows = P(AXES, None)
    in_specs = (P(("x", "zh"), ("zl", "y", "core")), rows, rows, P(), P(), P(), P())
    out_specs = (rows, rows, P(), P())
    return jax.shard_map(
        per_device, mesh=fine, in_specs=in_specs, out_specs=out_specs, check_vma=False
    )
```

```python
import jax
import jax.numpy as jnp
from jax import lax
from jax.experimental import pallas as pl
from jax.experimental.pallas import tpu as pltpu
from jax.sharding import Mesh, PartitionSpec as P

AXES = ("x", "zh", "zl", "y", "core")
SIZES = (4, 4, 4, 4, 2)
SWAP = [(0, 1), (1, 0)]
VMEM = pl.BlockSpec(memory_space=pltpu.VMEM)
SMEM = pl.BlockSpec(memory_space=pltpu.SMEM)
PARAMS = pltpu.CompilerParams(vmem_limit_bytes=32 * 1024 * 1024)


def exchange(parts, axes):
    return lax.all_to_all(parts, axes, 0, 0)


def gather(block, axes, count):
    return exchange(jnp.broadcast_to(block[None], (count, *block.shape)), axes)


def device_id(x, zh, zl, y, core):
    return (((x * 4 + zh) * 4 + zl) * 4 + y) * 2 + core


def turn_source(x, zh, zl, y):
    near = (1, 2, 3, 0) if zl < 2 else (2, 3, 0, 1)
    return zl, y, near[(zh - y) % 4], (y + 2 + x - zl) % 4


TURN = [
    (device_id(*turn_source(a, b, c, d), k), device_id(a, b, c, d, k))
    for a in range(4)
    for b in range(4)
    for c in range(4)
    for d in range(4)
    for k in range(2)
]


def multiply_kernel(pool, sibling, strip, rows, diag, out, rhs, full):
    core = lax.axis_index("core")
    shift = lax.axis_index("zl") - lax.axis_index("y") + 2
    depth = rhs.shape[0] // 2
    for side, which in ((0, core), (1, 1 - core)):
        for h in range(2):
            for j in range(4):
                start = side * depth + h * 256 + j * 64
                rhs[start : start + 64] = strip[(j + shift) & 3, 2 * which + h]
    for z in range(4):
        take = slice(z * 256, (z + 1) * 256)
        block = jnp.dot(
            pool[take], rhs[:depth], preferred_element_type=jnp.float32
        ) + jnp.dot(sibling[take], rhs[depth:], preferred_element_type=jnp.float32)
        out[take] = block
        for j in range(4):
            full[j, z * 64 : (z + 1) * 64] = block[j * 64 : (j + 1) * 64]
    term = jnp.zeros((256, 256), jnp.float32)
    for j in range(4):
        left, rest = rows[j], full[j]
        for _ in range(3):
            piece = rest.astype(jnp.bfloat16)
            rest = rest - piece.astype(jnp.float32)
            term = term + lax.dot_general(
                left, piece, (((0,), (0,)), ((), ())), preferred_element_type=jnp.float32
            )
    diag[0:256] = term[:, :128]
    diag[256:512] = term[:, 128:]


def split_kernel(mask, parts, stay, leave):
    core = lax.axis_index("core")
    own = -mask[lax.axis_index("zl")].astype(jnp.float32)
    column = (parts[0] + parts[1] + parts[2] + parts[3]) * own
    low = jnp.concatenate([column[0:32, 0:128], column[0:32, 128:256]])
    high = jnp.concatenate([column[32:64, 0:128], column[32:64, 128:256]])
    stay[...] = jnp.where(core == 0, low, high)
    leave[...] = jnp.where(core == 0, high, low)


def finish_kernel(total, stay, swapped, inv_one, inv_two, column_one, column_two, diag_one, diag_two):
    first = lax.axis_index("core") == 0
    own, other = total[...], swapped[0:512]
    own_column, other_column = stay[...], swapped[512:576]
    for swap, inv, diag, column in (
        (False, inv_one, diag_one, column_one),
        (True, inv_two, diag_two, column_two),
    ):
        pick = first != swap
        t = jnp.where(pick, own, other)
        c = jnp.where(pick, own_column, other_column).astype(jnp.bfloat16)
        diag[:, 0:128] = inv[:, 0:128] + t[0:256]
        diag[:, 128:256] = inv[:, 128:256] + t[256:512]
        column[:, 0:128] = c[0:32]
        column[:, 128:256] = c[32:64]


def call(kernel, outs, args, scratch=(), scalars=0):
    many = isinstance(outs, list)
    return pl.pallas_call(
        kernel,
        out_shape=outs,
        in_specs=[SMEM] * scalars + [VMEM] * (len(args) - scalars),
        out_specs=[VMEM] * len(outs) if many else VMEM,
        scratch_shapes=list(scratch),
        compiler_params=PARAMS,
    )(*args)


def per_device(
    inverse_pool, factor_one, factor_two, diag_inv_one, diag_inv_two, struct_one, struct_two
):
    row_count, width = factor_one.shape
    f32 = jnp.float32
    core = lax.axis_index("core")
    first = core == 0
    struct = jnp.where(first, struct_one, struct_two)
    mask = lax.dynamic_slice_in_dim(struct, lax.axis_index(("x", "zh")) * 4, 4)
    sibling_pool = lax.ppermute(inverse_pool, "core", SWAP)

    both = jnp.broadcast_to(
        jnp.stack([factor_one, factor_two])[None], (4, 2, row_count, width)
    ).reshape(8, row_count, width)
    rows = exchange(both, ("zl", "core")).reshape(4, 2 * row_count, width)
    rows = rows * mask.astype(jnp.bfloat16)[:, None, None]
    rows = lax.optimization_barrier(rows)
    strip = gather(lax.ppermute(rows, AXES, TURN), "x", 4)
    around = gather(rows, "y", 4).reshape(4, 256, width)

    diag, partial = call(
        multiply_kernel,
        [jax.ShapeDtypeStruct((512, 128), f32), jax.ShapeDtypeStruct((1024, width), f32)],
        (inverse_pool, sibling_pool, strip, around),
        [pltpu.VMEM((1024, width), jnp.bfloat16), pltpu.VMEM((4, 256, width), f32)],
    )
    product = lax.psum_scatter(partial, "zl", scatter_dimension=0, tiled=True)
    shard = jnp.sum(exchange(diag.reshape(64, 8, 128), ("x", "y", "zl")), axis=0)
    shard = jnp.sum(gather(shard, ("zh", "zl"), 16).reshape(4, 32, 128), axis=0)
    total = gather(shard, ("x", "y"), 16).reshape(512, 128)
    total, product = lax.optimization_barrier((total, product))
    half = jax.ShapeDtypeStruct((2 * row_count, 128), f32)
    parts = exchange(product.reshape(4, 2 * row_count, width), "y")
    stay, leave = call(split_kernel, [half, half], (mask, parts), scalars=1)
    swapped = lax.ppermute(jnp.concatenate([total, leave]), "core", SWAP)
    wide = jax.ShapeDtypeStruct((row_count, width), jnp.bfloat16)
    square = jax.ShapeDtypeStruct((width, width), f32)
    return tuple(
        call(
            finish_kernel,
            [wide, wide, square, square],
            (total, stay, swapped, diag_inv_one, diag_inv_two),
        )
    )


def solution(mesh):
    fine = Mesh(mesh.devices.reshape(SIZES), AXES)
    rows = P(AXES, None)
    in_specs = (P(("x", "zh"), ("zl", "y", "core")), rows, rows, P(), P(), P(), P())
    out_specs = (rows, rows, P(), P())
    return jax.shard_map(
        per_device, mesh=fine, in_specs=in_specs, out_specs=out_specs, check_vma=False
    )
```

```python
import jax
import jax.numpy as jnp
from jax import lax
from jax.experimental import pallas as pl
from jax.experimental.pallas import tpu as pltpu
from jax.sharding import Mesh, PartitionSpec as P

AXES = ("x", "zh", "zl", "y", "core")
SIZES = (4, 4, 4, 4, 2)
SWAP = [(0, 1), (1, 0)]
VMEM = pl.BlockSpec(memory_space=pltpu.VMEM)
SMEM = pl.BlockSpec(memory_space=pltpu.SMEM)
PARAMS = pltpu.CompilerParams(vmem_limit_bytes=32 * 1024 * 1024)


def exchange(parts, axes):
    return lax.all_to_all(parts, axes, 0, 0)


def gather(block, axes, count):
    return exchange(jnp.broadcast_to(block[None], (count, *block.shape)), axes)


def pair(block, axis, flip):
    return lax.ppermute(block, axis, [(i, i ^ flip) for i in range(4)])


def device_id(x, zh, zl, y, core):
    return (((x * 4 + zh) * 4 + zl) * 4 + y) * 2 + core


def turn_source(x, zh, zl, y):
    near = (1, 2, 3, 0) if zl < 2 else (2, 3, 0, 1)
    return zl, y, near[(zh - y) % 4], (y + 2 + x - zl) % 4


TURN = [
    (device_id(*turn_source(a, b, c, d), k), device_id(a, b, c, d, k))
    for a in range(4)
    for b in range(4)
    for c in range(4)
    for d in range(4)
    for k in range(2)
]


def multiply_kernel(pool, sibling, strip, rows, diag, keep, send, rhs, full):
    core, y = lax.axis_index("core"), lax.axis_index("y")
    shift = lax.axis_index("zl") - y + 2
    depth = rhs.shape[0] // 2
    for side, which in ((0, core), (1, 1 - core)):
        for h in range(2):
            for j in range(4):
                start = side * depth + h * 256 + j * 64
                rhs[start : start + 64] = strip[(j + shift) & 3, 2 * which + h]
    for z in range(4):
        take = slice(z * 256, (z + 1) * 256)
        block = jnp.dot(
            pool[take], rhs[:depth], preferred_element_type=jnp.float32
        ) + jnp.dot(sibling[take], rhs[depth:], preferred_element_type=jnp.float32)
        for j in range(4):
            full[j, z * 64 : (z + 1) * 64] = block[j * 64 : (j + 1) * 64]
    term = jnp.zeros((256, 256), jnp.float32)
    for j in range(4):
        left, rest = rows[j], full[j]
        for _ in range(3):
            piece = rest.astype(jnp.bfloat16)
            rest = rest - piece.astype(jnp.float32)
            term = term + lax.dot_general(
                left, piece, (((0,), (0,)), ((), ())), preferred_element_type=jnp.float32
            )
    diag[0:256] = term[:, :128]
    diag[256:512] = term[:, 128:]
    keep[0], keep[1] = full[y], full[y ^ 3]
    send[0], send[1] = full[y ^ 1], full[y ^ 2]


def half_kernel(kept, came, keep, send):
    keep[...] = kept[0] + came[0]
    send[...] = kept[1] + came[1]


def chunk_kernel(kept, came, keep, send, full):
    zl = lax.axis_index("zl")
    for z in range(4):
        full[z] = kept[z * 64 : (z + 1) * 64] + came[z * 64 : (z + 1) * 64]
    keep[0], keep[1] = full[zl], full[zl ^ 2]
    send[0], send[1] = full[zl ^ 1], full[zl ^ 3]


def split_kernel(mask, kept, came, stay, leave):
    core = lax.axis_index("core")
    own = -mask[lax.axis_index("zl")].astype(jnp.float32)
    column = (kept[...] + came[...]) * own
    low = jnp.concatenate([column[0:32, 0:128], column[0:32, 128:256]])
    high = jnp.concatenate([column[32:64, 0:128], column[32:64, 128:256]])
    stay[...] = jnp.where(core == 0, low, high)
    leave[...] = jnp.where(core == 0, high, low)


def finish_kernel(total, stay, swapped, inv_one, inv_two, column_one, column_two, diag_one, diag_two):
    first = lax.axis_index("core") == 0
    own, other = total[...], swapped[0:512]
    own_column, other_column = stay[...], swapped[512:576]
    for swap, inv, diag, column in (
        (False, inv_one, diag_one, column_one),
        (True, inv_two, diag_two, column_two),
    ):
        pick = first != swap
        t = jnp.where(pick, own, other)
        c = jnp.where(pick, own_column, other_column).astype(jnp.bfloat16)
        diag[:, 0:128] = inv[:, 0:128] + t[0:256]
        diag[:, 128:256] = inv[:, 128:256] + t[256:512]
        column[:, 0:128] = c[0:32]
        column[:, 128:256] = c[32:64]


def call(kernel, outs, args, scratch=(), scalars=0):
    many = isinstance(outs, list)
    return pl.pallas_call(
        kernel,
        out_shape=outs,
        in_specs=[SMEM] * scalars + [VMEM] * (len(args) - scalars),
        out_specs=[VMEM] * len(outs) if many else VMEM,
        scratch_shapes=list(scratch),
        compiler_params=PARAMS,
    )(*args)


def per_device(
    inverse_pool, factor_one, factor_two, diag_inv_one, diag_inv_two, struct_one, struct_two
):
    row_count, width = factor_one.shape
    f32 = jnp.float32
    core = lax.axis_index("core")
    first = core == 0
    struct = jnp.where(first, struct_one, struct_two)
    mask = lax.dynamic_slice_in_dim(struct, lax.axis_index(("x", "zh")) * 4, 4)
    sibling_pool = lax.ppermute(inverse_pool, "core", SWAP)

    both = jnp.broadcast_to(
        jnp.stack([factor_one, factor_two])[None], (4, 2, row_count, width)
    ).reshape(8, row_count, width)
    rows = exchange(both, ("zl", "core")).reshape(4, 2 * row_count, width)
    rows = rows * mask.astype(jnp.bfloat16)[:, None, None]
    rows = lax.optimization_barrier(rows)
    strip = gather(lax.ppermute(rows, AXES, TURN), "x", 4)
    around = gather(rows, "y", 4).reshape(4, 256, width)

    def buffers(*shapes):
        return [jax.ShapeDtypeStruct(shape, f32) for shape in shapes]

    chunk = 2 * row_count
    diag, keep, send = call(
        multiply_kernel,
        buffers((512, 128), (2, 256, width), (2, 256, width)),
        (inverse_pool, sibling_pool, strip, around),
        [pltpu.VMEM((1024, width), jnp.bfloat16), pltpu.VMEM((4, 256, width), f32)],
    )
    shard = jnp.sum(exchange(diag.reshape(64, 8, 128), ("x", "y", "zl")), axis=0)
    came = pair(send, "y", 1)
    keep, send = call(half_kernel, buffers((256, width), (256, width)), (keep, came))
    shard, keep, send = lax.optimization_barrier((shard, keep, send))
    shard = jnp.sum(gather(shard, ("zh", "zl"), 16).reshape(4, 32, 128), axis=0)
    came = pair(send, "y", 3)
    keep, send = call(
        chunk_kernel,
        buffers((2, chunk, width), (2, chunk, width)),
        (keep, came),
        [pltpu.VMEM((4, chunk, width), f32)],
    )
    came = pair(send, "zl", 1)
    shard, keep, came = lax.optimization_barrier((shard, keep, came))
    keep, send = call(half_kernel, buffers((chunk, width), (chunk, width)), (keep, came))
    came = pair(send, "zl", 2)
    stay, leave = call(
        split_kernel, buffers((chunk, 128), (chunk, 128)), (mask, keep, came), scalars=1
    )
    total = gather(shard, ("x", "y"), 16).reshape(512, 128)
    swapped = lax.ppermute(jnp.concatenate([total, leave]), "core", SWAP)
    wide = jax.ShapeDtypeStruct((row_count, width), jnp.bfloat16)
    square = jax.ShapeDtypeStruct((width, width), f32)
    return tuple(
        call(
            finish_kernel,
            [wide, wide, square, square],
            (total, stay, swapped, diag_inv_one, diag_inv_two),
        )
    )


def solution(mesh):
    fine = Mesh(mesh.devices.reshape(SIZES), AXES)
    rows = P(AXES, None)
    in_specs = (P(("x", "zh"), ("zl", "y", "core")), rows, rows, P(), P(), P(), P())
    out_specs = (rows, rows, P(), P())
    return jax.shard_map(
        per_device, mesh=fine, in_specs=in_specs, out_specs=out_specs, check_vma=False
    )
```

```python
import jax
import jax.numpy as jnp
from jax import lax
from jax.experimental import pallas as pl
from jax.experimental.pallas import tpu as pltpu
from jax.sharding import Mesh, PartitionSpec as P

AXES = ("x", "zh", "zl", "y", "core")
SIZES = (4, 4, 4, 4, 2)
SWAP = [(0, 1), (1, 0)]
VMEM = pl.BlockSpec(memory_space=pltpu.VMEM)
SMEM = pl.BlockSpec(memory_space=pltpu.SMEM)
PARAMS = pltpu.CompilerParams(vmem_limit_bytes=32 * 1024 * 1024)


def exchange(parts, axes):
    return lax.all_to_all(parts, axes, 0, 0)


def gather(block, axes, count):
    return exchange(jnp.broadcast_to(block[None], (count, *block.shape)), axes)


def rotate(parts, axis):
    return [parts[0]] + [
        lax.ppermute(parts[s], axis, [(i, (i + s) % 4) for i in range(4)]) for s in (1, 2, 3)
    ]


def device_id(x, zh, zl, y, core):
    return (((x * 4 + zh) * 4 + zl) * 4 + y) * 2 + core


def turn_source(x, zh, zl, y):
    near = (1, 2, 3, 0) if zl < 2 else (2, 3, 0, 1)
    return zl, y, near[(zh - y) % 4], (y + 2 + x - zl) % 4


TURN = [
    (device_id(*turn_source(a, b, c, d), k), device_id(a, b, c, d, k))
    for a in range(4)
    for b in range(4)
    for c in range(4)
    for d in range(4)
    for k in range(2)
]


def multiply_kernel(pool, sibling, strip, rows, diag, out0, out1, out2, out3, rhs, full):
    core, y = lax.axis_index("core"), lax.axis_index("y")
    shift = lax.axis_index("zl") - y + 2
    depth = rhs.shape[0] // 2
    for side, which in ((0, core), (1, 1 - core)):
        for h in range(2):
            for j in range(4):
                start = side * depth + h * 256 + j * 64
                rhs[start : start + 64] = strip[(j + shift) & 3, 2 * which + h]
    for z in range(4):
        take = slice(z * 256, (z + 1) * 256)
        block = jnp.dot(
            pool[take], rhs[:depth], preferred_element_type=jnp.float32
        ) + jnp.dot(sibling[take], rhs[depth:], preferred_element_type=jnp.float32)
        for j in range(4):
            full[j, z * 64 : (z + 1) * 64] = block[j * 64 : (j + 1) * 64]
    term = jnp.zeros((256, 256), jnp.float32)
    for j in range(4):
        left, rest = rows[j], full[j]
        for _ in range(3):
            piece = rest.astype(jnp.bfloat16)
            rest = rest - piece.astype(jnp.float32)
            term = term + lax.dot_general(
                left, piece, (((0,), (0,)), ((), ())), preferred_element_type=jnp.float32
            )
    diag[0:128] = term[:128, :128]
    diag[128:256] = term[:128, 128:]
    diag[256:384] = term[128:, 128:]
    for hop, out in enumerate((out0, out1, out2, out3)):
        out[...] = full[(y + hop) & 3]


def turn_kernel(in0, in1, in2, in3, out0, out1, out2, out3, full):
    zl = lax.axis_index("zl")
    full[...] = in0[...] + in1[...] + in2[...] + in3[...]
    for hop, out in enumerate((out0, out1, out2, out3)):
        out[...] = full[pl.ds(pl.multiple_of(((zl + hop) & 3) * 64, 64), 64)]


def split_kernel(mask, in0, in1, in2, in3, stay, leave):
    core = lax.axis_index("core")
    own = -mask[lax.axis_index("zl")].astype(jnp.float32)
    column = (in0[...] + in1[...] + in2[...] + in3[...]) * own
    low = jnp.concatenate([column[0:32, 0:128], column[0:32, 128:256]])
    high = jnp.concatenate([column[32:64, 0:128], column[32:64, 128:256]])
    stay[...] = jnp.where(core == 0, low, high)
    leave[...] = jnp.where(core == 0, high, low)


def finish_kernel(total, stay, swapped, inv_one, inv_two, column_one, column_two, diag_one, diag_two):
    first = lax.axis_index("core") == 0
    own, other = total[...], swapped[0:384]
    own_column, other_column = stay[...], swapped[384:448]
    for swap, inv, diag, column in (
        (False, inv_one, diag_one, column_one),
        (True, inv_two, diag_two, column_two),
    ):
        pick = first != swap
        t = jnp.where(pick, own, other)
        c = jnp.where(pick, own_column, other_column).astype(jnp.bfloat16)
        diag[0:128, 0:128] = inv[0:128, 0:128] + t[0:128]
        diag[0:128, 128:256] = inv[0:128, 128:256] + t[128:256]
        diag[128:256, 0:128] = inv[128:256, 0:128] + t[128:256].T
        diag[128:256, 128:256] = inv[128:256, 128:256] + t[256:384]
        column[:, 0:128] = c[0:32]
        column[:, 128:256] = c[32:64]


def call(kernel, outs, args, scratch=(), scalars=0):
    many = isinstance(outs, list)
    return pl.pallas_call(
        kernel,
        out_shape=outs,
        in_specs=[SMEM] * scalars + [VMEM] * (len(args) - scalars),
        out_specs=[VMEM] * len(outs) if many else VMEM,
        scratch_shapes=list(scratch),
        compiler_params=PARAMS,
    )(*args)


def per_device(
    inverse_pool, factor_one, factor_two, diag_inv_one, diag_inv_two, struct_one, struct_two
):
    row_count, width = factor_one.shape
    f32 = jnp.float32
    core = lax.axis_index("core")
    first = core == 0
    struct = jnp.where(first, struct_one, struct_two)
    mask = lax.dynamic_slice_in_dim(struct, lax.axis_index(("x", "zh")) * 4, 4)
    sibling_pool = lax.ppermute(inverse_pool, "core", SWAP)

    both = jnp.broadcast_to(
        jnp.stack([factor_one, factor_two])[None], (4, 2, row_count, width)
    ).reshape(8, row_count, width)
    rows = exchange(both, ("zl", "core")).reshape(4, 2 * row_count, width)
    rows = rows * mask.astype(jnp.bfloat16)[:, None, None]
    rows = lax.optimization_barrier(rows)
    strip = gather(lax.ppermute(rows, AXES, TURN), "x", 4)
    around = gather(rows, "y", 4).reshape(4, 256, width)

    quarter = jax.ShapeDtypeStruct((256, width), f32)
    diag, *parts = call(
        multiply_kernel,
        [jax.ShapeDtypeStruct((384, 128), f32)] + [quarter] * 4,
        (inverse_pool, sibling_pool, strip, around),
        [pltpu.VMEM((1024, width), jnp.bfloat16), pltpu.VMEM((4, 256, width), f32)],
    )
    shard = jnp.sum(exchange(diag.reshape(16, 24, 128), ("x", "y")), axis=0)
    parts = rotate(parts, "y")
    shard = jnp.sum(gather(shard, ("zh", "zl"), 16), axis=0)
    parts = call(
        turn_kernel,
        [jax.ShapeDtypeStruct((2 * row_count, width), f32)] * 4,
        parts,
        [pltpu.VMEM((256, width), f32)],
    )
    parts = rotate(parts, "zl")
    half = jax.ShapeDtypeStruct((2 * row_count, 128), f32)
    stay, leave = call(split_kernel, [half, half], (mask, *parts), scalars=1)
    total = gather(shard, ("x", "y"), 16).reshape(384, 128)
    swapped = lax.ppermute(jnp.concatenate([total, leave]), "core", SWAP)
    wide = jax.ShapeDtypeStruct((row_count, width), jnp.bfloat16)
    square = jax.ShapeDtypeStruct((width, width), f32)
    return tuple(
        call(
            finish_kernel,
            [wide, wide, square, square],
            (total, stay, swapped, diag_inv_one, diag_inv_two),
        )
    )


def solution(mesh):
    fine = Mesh(mesh.devices.reshape(SIZES), AXES)
    rows = P(AXES, None)
    in_specs = (P(("x", "zh"), ("zl", "y", "core")), rows, rows, P(), P(), P(), P())
    out_specs = (rows, rows, P(), P())
    return jax.shard_map(
        per_device, mesh=fine, in_specs=in_specs, out_specs=out_specs, check_vma=False
    )
```

```python
import jax
import jax.numpy as jnp
from jax import lax
from jax.experimental import pallas as pl
from jax.experimental.pallas import tpu as pltpu
from jax.sharding import Mesh, PartitionSpec as P

AXES = ("x", "zh", "zl", "y", "core")
SIZES = (4, 4, 4, 4, 2)
SWAP = [(0, 1), (1, 0)]
VMEM = pl.BlockSpec(memory_space=pltpu.VMEM)
SMEM = pl.BlockSpec(memory_space=pltpu.SMEM)
PARAMS = pltpu.CompilerParams(vmem_limit_bytes=32 * 1024 * 1024)


def exchange(parts, axes):
    return lax.all_to_all(parts, axes, 0, 0)


def gather(block, axes, count):
    return exchange(jnp.broadcast_to(block[None], (count, *block.shape)), axes)


def rotate(parts, axis):
    return [parts[0]] + [
        lax.ppermute(parts[s], axis, [(i, (i + s) % 4) for i in range(4)]) for s in (1, 2, 3)
    ]


def device_id(x, zh, zl, y, core):
    return (((x * 4 + zh) * 4 + zl) * 4 + y) * 2 + core


def turn_source(x, zh, zl, y):
    near = (1, 2, 3, 0) if zl < 2 else (2, 3, 0, 1)
    return zl, y, near[(zh - y) % 4], (y + 2 + x - zl) % 4


TURN = [
    (device_id(*turn_source(a, b, c, d), k), device_id(a, b, c, d, k))
    for a in range(4)
    for b in range(4)
    for c in range(4)
    for d in range(4)
    for k in range(2)
]


def multiply_kernel(pool, sibling, strip, rows, diag, out0, out1, out2, out3, rhs, full):
    core, y = lax.axis_index("core"), lax.axis_index("y")
    shift = lax.axis_index("zl") - y + 2
    depth = rhs.shape[0] // 2
    for side, which in ((0, core), (1, 1 - core)):
        for h in range(2):
            for j in range(4):
                start = side * depth + h * 256 + j * 64
                rhs[start : start + 64] = strip[(j + shift) & 3, 2 * which + h]
    for z in range(4):
        take = slice(z * 256, (z + 1) * 256)
        block = jnp.dot(
            pool[take], rhs[:depth], preferred_element_type=jnp.float32
        ) + jnp.dot(sibling[take], rhs[depth:], preferred_element_type=jnp.float32)
        for j in range(4):
            full[j, z * 64 : (z + 1) * 64] = block[j * 64 : (j + 1) * 64]
    term = jnp.zeros((256, 256), jnp.float32)
    for j in range(4):
        left, rest = rows[j], full[j]
        for _ in range(3):
            piece = rest.astype(jnp.bfloat16)
            rest = rest - piece.astype(jnp.float32)
            term = term + lax.dot_general(
                left, piece, (((0,), (0,)), ((), ())), preferred_element_type=jnp.float32
            )
    diag[0:256] = term[:, :128]
    diag[256:512] = term[:, 128:]
    for hop, out in enumerate((out0, out1, out2, out3)):
        out[...] = full[(y + hop) & 3]


def join_kernel(in0, in1, in2, in3, quarter, joined):
    total = in0[...] + in1[...] + in2[...] + in3[...]
    for z in range(4):
        joined[z, 0:64] = total[z * 64 : (z + 1) * 64, :128]
        joined[z, 64:128] = total[z * 64 : (z + 1) * 64, 128:]
        joined[z, 128:136] = quarter[...]


def split_kernel(mask, parts, shards, stay, leave):
    core = lax.axis_index("core")
    own = -mask[lax.axis_index("zl")].astype(jnp.float32)
    for i in range(16):
        for z in range(4):
            shards[i, z * 8 : (z + 1) * 8] = parts[z, 128:136]
    column = (parts[0, 0:128] + parts[1, 0:128] + parts[2, 0:128] + parts[3, 0:128]) * own
    low = jnp.concatenate([column[0:32], column[64:96]])
    high = jnp.concatenate([column[32:64], column[96:128]])
    stay[...] = jnp.where(core == 0, low, high)
    leave[...] = jnp.where(core == 0, high, low)


def finish_kernel(total, stay, swapped, inv_one, inv_two, column_one, column_two, diag_one, diag_two):
    first = lax.axis_index("core") == 0
    own, other = total[...], swapped[0:512]
    own_column, other_column = stay[...], swapped[512:576]
    for swap, inv, diag, column in (
        (False, inv_one, diag_one, column_one),
        (True, inv_two, diag_two, column_two),
    ):
        pick = first != swap
        t = jnp.where(pick, own, other)
        c = jnp.where(pick, own_column, other_column).astype(jnp.bfloat16)
        diag[:, 0:128] = inv[:, 0:128] + t[0:256]
        diag[:, 128:256] = inv[:, 128:256] + t[256:512]
        column[:, 0:128] = c[0:32]
        column[:, 128:256] = c[32:64]


def call(kernel, outs, args, scratch=(), scalars=0):
    many = isinstance(outs, list)
    return pl.pallas_call(
        kernel,
        out_shape=outs,
        in_specs=[SMEM] * scalars + [VMEM] * (len(args) - scalars),
        out_specs=[VMEM] * len(outs) if many else VMEM,
        scratch_shapes=list(scratch),
        compiler_params=PARAMS,
    )(*args)


def per_device(
    inverse_pool, factor_one, factor_two, diag_inv_one, diag_inv_two, struct_one, struct_two
):
    row_count, width = factor_one.shape
    f32 = jnp.float32
    core = lax.axis_index("core")
    first = core == 0
    struct = jnp.where(first, struct_one, struct_two)
    mask = lax.dynamic_slice_in_dim(struct, lax.axis_index(("x", "zh")) * 4, 4)
    sibling_pool = lax.ppermute(inverse_pool, "core", SWAP)

    both = jnp.broadcast_to(
        jnp.stack([factor_one, factor_two])[None], (4, 2, row_count, width)
    ).reshape(8, row_count, width)
    rows = exchange(both, ("zl", "core")).reshape(4, 2 * row_count, width)
    rows = rows * mask.astype(jnp.bfloat16)[:, None, None]
    rows = lax.optimization_barrier(rows)
    strip = gather(lax.ppermute(rows, AXES, TURN), "x", 4)
    around = gather(rows, "y", 4).reshape(4, 256, width)

    quarter = jax.ShapeDtypeStruct((256, width), f32)
    diag, *parts = call(
        multiply_kernel,
        [jax.ShapeDtypeStruct((512, 128), f32)] + [quarter] * 4,
        (inverse_pool, sibling_pool, strip, around),
        [pltpu.VMEM((1024, width), jnp.bfloat16), pltpu.VMEM((4, 256, width), f32)],
    )
    def buffers(*shapes):
        return [jax.ShapeDtypeStruct(shape, f32) for shape in shapes]

    shard = jnp.sum(exchange(diag.reshape(16, 32, 128), ("x", "y")), axis=0)
    parts = rotate(parts, "y")
    quarters = jnp.broadcast_to(shard.reshape(1, 4, 8, 128), (4, 4, 8, 128)).reshape(16, 8, 128)
    quarter = jnp.sum(exchange(quarters, ("zh", "zl")), axis=0)
    (joined,) = call(join_kernel, buffers((4, 136, 128)), (*parts, quarter))
    half = (2 * row_count, 128)
    shards, stay, leave = call(
        split_kernel, buffers((16, 32, 128), half, half), (mask, exchange(joined, "zl")), scalars=1
    )
    total = exchange(shards, ("x", "y")).reshape(512, 128)
    swapped = lax.ppermute(jnp.concatenate([total, leave]), "core", SWAP)
    wide = jax.ShapeDtypeStruct((row_count, width), jnp.bfloat16)
    square = jax.ShapeDtypeStruct((width, width), f32)
    return tuple(
        call(
            finish_kernel,
            [wide, wide, square, square],
            (total, stay, swapped, diag_inv_one, diag_inv_two),
        )
    )


def solution(mesh):
    fine = Mesh(mesh.devices.reshape(SIZES), AXES)
    rows = P(AXES, None)
    in_specs = (P(("x", "zh"), ("zl", "y", "core")), rows, rows, P(), P(), P(), P())
    out_specs = (rows, rows, P(), P())
    return jax.shard_map(
        per_device, mesh=fine, in_specs=in_specs, out_specs=out_specs, check_vma=False
    )
```

```python
import jax
import jax.numpy as jnp
from jax import lax
from jax.experimental import pallas as pl
from jax.experimental.pallas import tpu as pltpu
from jax.sharding import Mesh, PartitionSpec as P

AXES = ("x", "zh", "zl", "y", "core")
SIZES = (4, 4, 4, 4, 2)
SWAP = [(0, 1), (1, 0)]
VMEM = pl.BlockSpec(memory_space=pltpu.VMEM)
SMEM = pl.BlockSpec(memory_space=pltpu.SMEM)
PARAMS = pltpu.CompilerParams(vmem_limit_bytes=32 * 1024 * 1024)


def exchange(parts, axes):
    return lax.all_to_all(parts, axes, 0, 0)


def gather(block, axes, count):
    return exchange(jnp.broadcast_to(block[None], (count, *block.shape)), axes)


def rotate(parts, axis):
    return [parts[0]] + [
        lax.ppermute(parts[s], axis, [(i, (i + s) % 4) for i in range(4)]) for s in (1, 2, 3)
    ]


def device_id(x, zh, zl, y, core):
    return (((x * 4 + zh) * 4 + zl) * 4 + y) * 2 + core


def turn_source(x, zh, zl, y):
    near = (1, 2, 3, 0) if zl < 2 else (2, 3, 0, 1)
    return zl, y, near[(zh - y) % 4], (y + 2 + x - zl) % 4


TURN = [
    (device_id(*turn_source(a, b, c, d), k), device_id(a, b, c, d, k))
    for a in range(4)
    for b in range(4)
    for c in range(4)
    for d in range(4)
    for k in range(2)
]


def multiply_kernel(pool, sibling, strip, rows, diag, out0, out1, out2, out3, rhs, full):
    core, y = lax.axis_index("core"), lax.axis_index("y")
    shift = lax.axis_index("zl") - y + 2
    depth = rhs.shape[0] // 2
    for side, which in ((0, core), (1, 1 - core)):
        for h in range(2):
            for j in range(4):
                start = side * depth + h * 256 + j * 64
                rhs[start : start + 64] = strip[(j + shift) & 3, 2 * which + h]
    for z in range(4):
        take = slice(z * 256, (z + 1) * 256)
        block = jnp.dot(
            pool[take], rhs[:depth], preferred_element_type=jnp.float32
        ) + jnp.dot(sibling[take], rhs[depth:], preferred_element_type=jnp.float32)
        for j in range(4):
            full[j, z * 64 : (z + 1) * 64] = block[j * 64 : (j + 1) * 64]
    term = jnp.zeros((256, 256), jnp.float32)
    for j in range(4):
        left, rest = rows[j], full[j]
        for _ in range(3):
            piece = rest.astype(jnp.bfloat16)
            rest = rest - piece.astype(jnp.float32)
            term = term + lax.dot_general(
                left, piece, (((0,), (0,)), ((), ())), preferred_element_type=jnp.float32
            )
    diag[0:256] = term[:, :128]
    diag[256:512] = term[:, 128:]
    for hop, out in enumerate((out0, out1, out2, out3)):
        out[...] = full[(y + hop) & 3]


def join_kernel(in0, in1, in2, in3, quarter, joined):
    total = in0[...] + in1[...] + in2[...] + in3[...]
    for z in range(4):
        joined[z, 0:64] = total[z * 64 : (z + 1) * 64, :128]
        joined[z, 64:128] = total[z * 64 : (z + 1) * 64, 128:]
        joined[z, 128:136] = quarter[...]


def split_kernel(mask, parts, shards, stay, leave):
    core = lax.axis_index("core")
    own = -mask[lax.axis_index("zl")].astype(jnp.float32)
    for i in range(16):
        for z in range(4):
            shards[i, z * 8 : (z + 1) * 8] = parts[z, 128:136]
    column = (parts[0, 0:128] + parts[1, 0:128] + parts[2, 0:128] + parts[3, 0:128]) * own
    low = jnp.concatenate([column[0:32], column[64:96]])
    high = jnp.concatenate([column[32:64], column[96:128]])
    stay[...] = jnp.where(core == 0, low, high)
    leave[...] = jnp.where(core == 0, high, low)


def finish_kernel(total, stay, swapped, inv_one, inv_two, column_one, column_two, diag_one, diag_two):
    first = lax.axis_index("core") == 0
    own, other = total[...], swapped[0:512]
    own_column, other_column = stay[...], swapped[512:576]
    for swap, inv, diag, column in (
        (False, inv_one, diag_one, column_one),
        (True, inv_two, diag_two, column_two),
    ):
        pick = first != swap
        t = jnp.where(pick, own, other)
        c = jnp.where(pick, own_column, other_column).astype(jnp.bfloat16)
        diag[:, 0:128] = inv[:, 0:128] + t[0:256]
        diag[:, 128:256] = inv[:, 128:256] + t[256:512]
        column[:, 0:128] = c[0:32]
        column[:, 128:256] = c[32:64]


def call(kernel, outs, args, scratch=(), scalars=0):
    many = isinstance(outs, list)
    return pl.pallas_call(
        kernel,
        out_shape=outs,
        in_specs=[SMEM] * scalars + [VMEM] * (len(args) - scalars),
        out_specs=[VMEM] * len(outs) if many else VMEM,
        scratch_shapes=list(scratch),
        compiler_params=PARAMS,
    )(*args)


def per_device(
    inverse_pool, factor_one, factor_two, diag_inv_one, diag_inv_two, struct_one, struct_two
):
    row_count, width = factor_one.shape
    f32 = jnp.float32
    core = lax.axis_index("core")
    first = core == 0
    struct = jnp.where(first, struct_one, struct_two)
    mask = lax.dynamic_slice_in_dim(struct, lax.axis_index(("x", "zh")) * 4, 4)
    sibling_pool = lax.ppermute(inverse_pool, "core", SWAP)

    both = jnp.broadcast_to(
        jnp.stack([factor_one, factor_two])[None], (4, 2, row_count, width)
    ).reshape(8, row_count, width)
    rows = exchange(both, ("zl", "core")).reshape(4, 2 * row_count, width)
    rows = rows * mask.astype(jnp.bfloat16)[:, None, None]
    rows = lax.optimization_barrier(rows)
    strip = gather(lax.ppermute(rows, AXES, TURN), "x", 4)
    around = gather(rows, "y", 4).reshape(4, 256, width)

    quarter = jax.ShapeDtypeStruct((256, width), f32)
    diag, *parts = call(
        multiply_kernel,
        [jax.ShapeDtypeStruct((512, 128), f32)] + [quarter] * 4,
        (inverse_pool, sibling_pool, strip, around),
        [pltpu.VMEM((1024, width), jnp.bfloat16), pltpu.VMEM((4, 256, width), f32)],
    )
    def buffers(*shapes):
        return [jax.ShapeDtypeStruct(shape, f32) for shape in shapes]

    shard = jnp.sum(exchange(diag.reshape(16, 32, 128), ("x", "y")), axis=0)
    parts = rotate(parts, "y")
    quarters = jnp.broadcast_to(shard.reshape(1, 4, 1, 8, 128), (4, 4, 2, 8, 128))
    quarters = exchange(quarters.reshape(16, 16, 128), ("zh", "zl"))
    quarter = jnp.sum(quarters[:, :8], axis=0)
    (joined,) = call(join_kernel, buffers((4, 136, 128)), (*parts, quarter))
    half = (2 * row_count, 128)
    shards, stay, leave = call(
        split_kernel, buffers((16, 32, 128), half, half), (mask, exchange(joined, "zl")), scalars=1
    )
    total = exchange(shards, ("x", "y")).reshape(512, 128)
    swapped = lax.ppermute(jnp.concatenate([total, leave]), "core", SWAP)
    wide = jax.ShapeDtypeStruct((row_count, width), jnp.bfloat16)
    square = jax.ShapeDtypeStruct((width, width), f32)
    return tuple(
        call(
            finish_kernel,
            [wide, wide, square, square],
            (total, stay, swapped, diag_inv_one, diag_inv_two),
        )
    )


def solution(mesh):
    fine = Mesh(mesh.devices.reshape(SIZES), AXES)
    rows = P(AXES, None)
    in_specs = (P(("x", "zh"), ("zl", "y", "core")), rows, rows, P(), P(), P(), P())
    out_specs = (rows, rows, P(), P())
    return jax.shard_map(
        per_device, mesh=fine, in_specs=in_specs, out_specs=out_specs, check_vma=False
    )
```

```python
import jax
import jax.numpy as jnp
from jax import lax
from jax.experimental import pallas as pl
from jax.experimental.pallas import tpu as pltpu
from jax.sharding import Mesh, PartitionSpec as P

AXES = ("x", "zh", "zl", "y", "core")
SIZES = (4, 4, 4, 4, 2)
SWAP = [(0, 1), (1, 0)]
VMEM = pl.BlockSpec(memory_space=pltpu.VMEM)
SMEM = pl.BlockSpec(memory_space=pltpu.SMEM)
PARAMS = pltpu.CompilerParams(vmem_limit_bytes=32 * 1024 * 1024)


def exchange(parts, axes):
    return lax.all_to_all(parts, axes, 0, 0)


def gather(block, axes, count):
    return exchange(jnp.broadcast_to(block[None], (count, *block.shape)), axes)


def rotate(parts, axis):
    return [parts[0]] + [
        lax.ppermute(parts[s], axis, [(i, (i + s) % 4) for i in range(4)]) for s in (1, 2, 3)
    ]


def device_id(x, zh, zl, y, core):
    return (((x * 4 + zh) * 4 + zl) * 4 + y) * 2 + core


def turn_source(x, zh, zl, y):
    near = (1, 2, 3, 0) if zl < 2 else (2, 3, 0, 1)
    return zl, y, near[(zh - y) % 4], (y + 2 + x - zl) % 4


TURN = [
    (device_id(*turn_source(a, b, c, d), k), device_id(a, b, c, d, k))
    for a in range(4)
    for b in range(4)
    for c in range(4)
    for d in range(4)
    for k in range(2)
]


def multiply_kernel(pool, sibling, strip, rows0, rows1, rows2, rows3, diag, out0, out1, out2, out3, rhs, full):
    core, y = lax.axis_index("core"), lax.axis_index("y")
    shift = lax.axis_index("zl") - y + 2
    depth = rhs.shape[0] // 2
    for side, which in ((0, core), (1, 1 - core)):
        for h in range(2):
            for j in range(4):
                start = side * depth + h * 256 + j * 64
                rhs[start : start + 64] = strip[(j + shift) & 3, 2 * which + h]
    for z in range(4):
        take = slice(z * 256, (z + 1) * 256)
        block = jnp.dot(
            pool[take], rhs[:depth], preferred_element_type=jnp.float32
        ) + jnp.dot(sibling[take], rhs[depth:], preferred_element_type=jnp.float32)
        for j in range(4):
            full[j, z * 64 : (z + 1) * 64] = block[j * 64 : (j + 1) * 64]
    term = jnp.zeros((256, 256), jnp.float32)
    for hop, rows in enumerate((rows0, rows1, rows2, rows3)):
        left, rest = rows[...], full[(y - hop) & 3]
        for _ in range(3):
            piece = rest.astype(jnp.bfloat16)
            rest = rest - piece.astype(jnp.float32)
            term = term + lax.dot_general(
                left, piece, (((0,), (0,)), ((), ())), preferred_element_type=jnp.float32
            )
    diag[0:128] = term[:128, :128]
    diag[128:256] = term[:128, 128:]
    diag[256:384] = term[128:, 128:]
    for hop, out in enumerate((out0, out1, out2, out3)):
        out[...] = full[(y + hop) & 3]


def turn_kernel(in0, in1, in2, in3, out0, out1, out2, out3, full):
    zl = lax.axis_index("zl")
    full[...] = in0[...] + in1[...] + in2[...] + in3[...]
    for hop, out in enumerate((out0, out1, out2, out3)):
        out[...] = full[pl.ds(pl.multiple_of(((zl + hop) & 3) * 64, 64), 64)]


def split_kernel(mask, in0, in1, in2, in3, stay, leave):
    core = lax.axis_index("core")
    own = -mask[lax.axis_index("zl")].astype(jnp.float32)
    column = (in0[...] + in1[...] + in2[...] + in3[...]) * own
    low = jnp.concatenate([column[0:32, 0:128], column[0:32, 128:256]])
    high = jnp.concatenate([column[32:64, 0:128], column[32:64, 128:256]])
    stay[...] = jnp.where(core == 0, low, high)
    leave[...] = jnp.where(core == 0, high, low)


def finish_kernel(total, stay, swapped, inv_one, inv_two, column_one, column_two, diag_one, diag_two):
    first = lax.axis_index("core") == 0
    own, other = total[...], swapped[0:384]
    own_column, other_column = stay[...], swapped[384:448]
    for swap, inv, diag, column in (
        (False, inv_one, diag_one, column_one),
        (True, inv_two, diag_two, column_two),
    ):
        pick = first != swap
        t = jnp.where(pick, own, other)
        c = jnp.where(pick, own_column, other_column).astype(jnp.bfloat16)
        diag[0:128, 0:128] = inv[0:128, 0:128] + t[0:128]
        diag[0:128, 128:256] = inv[0:128, 128:256] + t[128:256]
        diag[128:256, 0:128] = inv[128:256, 0:128] + t[128:256].T
        diag[128:256, 128:256] = inv[128:256, 128:256] + t[256:384]
        column[:, 0:128] = c[0:32]
        column[:, 128:256] = c[32:64]


def call(kernel, outs, args, scratch=(), scalars=0):
    many = isinstance(outs, list)
    return pl.pallas_call(
        kernel,
        out_shape=outs,
        in_specs=[SMEM] * scalars + [VMEM] * (len(args) - scalars),
        out_specs=[VMEM] * len(outs) if many else VMEM,
        scratch_shapes=list(scratch),
        compiler_params=PARAMS,
    )(*args)


def per_device(
    inverse_pool, factor_one, factor_two, diag_inv_one, diag_inv_two, struct_one, struct_two
):
    row_count, width = factor_one.shape
    f32 = jnp.float32
    core = lax.axis_index("core")
    first = core == 0
    struct = jnp.where(first, struct_one, struct_two)
    mask = lax.dynamic_slice_in_dim(struct, lax.axis_index(("x", "zh")) * 4, 4)
    sibling_pool = lax.ppermute(inverse_pool, "core", SWAP)

    both = jnp.broadcast_to(
        jnp.stack([factor_one, factor_two])[None], (4, 2, row_count, width)
    ).reshape(8, row_count, width)
    rows = exchange(both, ("zl", "core")).reshape(4, 2 * row_count, width)
    rows = rows * mask.astype(jnp.bfloat16)[:, None, None]
    rows = lax.optimization_barrier(rows)
    turned, rows = lax.optimization_barrier((lax.ppermute(rows, AXES, TURN), rows))
    strip = gather(turned, "x", 4)
    flat = rows.reshape(256, width)
    around = rotate([flat] * 4, "y")

    quarter = jax.ShapeDtypeStruct((256, width), f32)
    diag, *parts = call(
        multiply_kernel,
        [jax.ShapeDtypeStruct((384, 128), f32)] + [quarter] * 4,
        (inverse_pool, sibling_pool, strip, *around),
        [pltpu.VMEM((1024, width), jnp.bfloat16), pltpu.VMEM((4, 256, width), f32)],
    )
    shard = jnp.sum(exchange(diag.reshape(16, 24, 128), ("x", "y")), axis=0)
    parts = rotate(parts, "y")
    shard = jnp.sum(gather(shard, ("zh", "zl"), 16), axis=0)
    parts = call(
        turn_kernel,
        [jax.ShapeDtypeStruct((2 * row_count, width), f32)] * 4,
        parts,
        [pltpu.VMEM((256, width), f32)],
    )
    parts = rotate(parts, "zl")
    half = jax.ShapeDtypeStruct((2 * row_count, 128), f32)
    stay, leave = call(split_kernel, [half, half], (mask, *parts), scalars=1)
    total = gather(shard, ("x", "y"), 16).reshape(384, 128)
    swapped = lax.ppermute(jnp.concatenate([total, leave]), "core", SWAP)
    wide = jax.ShapeDtypeStruct((row_count, width), jnp.bfloat16)
    square = jax.ShapeDtypeStruct((width, width), f32)
    return tuple(
        call(
            finish_kernel,
            [wide, wide, square, square],
            (total, stay, swapped, diag_inv_one, diag_inv_two),
        )
    )


def solution(mesh):
    fine = Mesh(mesh.devices.reshape(SIZES), AXES)
    rows = P(AXES, None)
    in_specs = (P(("x", "zh"), ("zl", "y", "core")), rows, rows, P(), P(), P(), P())
    out_specs = (rows, rows, P(), P())
    return jax.shard_map(
        per_device, mesh=fine, in_specs=in_specs, out_specs=out_specs, check_vma=False
    )
```

```python
import jax
import jax.numpy as jnp
from jax import lax
from jax.experimental import pallas as pl
from jax.experimental.pallas import tpu as pltpu
from jax.sharding import Mesh, PartitionSpec as P

AXES = ("x", "zh", "zl", "y", "core")
SIZES = (4, 4, 4, 4, 2)
SWAP = [(0, 1), (1, 0)]
VMEM = pl.BlockSpec(memory_space=pltpu.VMEM)
SMEM = pl.BlockSpec(memory_space=pltpu.SMEM)
PARAMS = pltpu.CompilerParams(vmem_limit_bytes=32 * 1024 * 1024)


def exchange(parts, axes):
    return lax.all_to_all(parts, axes, 0, 0)


def gather(block, axes, count):
    return exchange(jnp.broadcast_to(block[None], (count, *block.shape)), axes)


def rotate(parts, axis):
    return [parts[0]] + [
        lax.ppermute(parts[s], axis, [(i, (i + s) % 4) for i in range(4)]) for s in (1, 2, 3)
    ]


def device_id(x, zh, zl, y, core):
    return (((x * 4 + zh) * 4 + zl) * 4 + y) * 2 + core


def turn_source(x, zh, zl, y):
    near = (1, 2, 3, 0) if zl < 2 else (2, 3, 0, 1)
    return zl, y, near[(zh - y) % 4], (y + 2 + x - zl) % 4


TURN = [
    (device_id(*turn_source(a, b, c, d), k), device_id(a, b, c, d, k))
    for a in range(4)
    for b in range(4)
    for c in range(4)
    for d in range(4)
    for k in range(2)
]


def multiply_kernel(pool, sibling, strip, rows, diag, out0, out1, out2, out3, rhs, full):
    core, y = lax.axis_index("core"), lax.axis_index("y")
    shift = lax.axis_index("zl") - y + 2
    depth = rhs.shape[0] // 2
    for side, which in ((0, core), (1, 1 - core)):
        for h in range(2):
            for j in range(4):
                start = side * depth + h * 256 + j * 64
                rhs[start : start + 64] = strip[(j + shift) & 3, 2 * which + h]
    for z in range(4):
        take = slice(z * 256, (z + 1) * 256)
        block = jnp.dot(
            pool[take], rhs[:depth], preferred_element_type=jnp.float32
        ) + jnp.dot(sibling[take], rhs[depth:], preferred_element_type=jnp.float32)
        for j in range(4):
            full[j, z * 64 : (z + 1) * 64] = block[j * 64 : (j + 1) * 64]
    term = jnp.zeros((256, 256), jnp.float32)
    for j in range(4):
        left, rest = rows[j], full[j]
        for _ in range(3):
            piece = rest.astype(jnp.bfloat16)
            rest = rest - piece.astype(jnp.float32)
            term = term + lax.dot_general(
                left, piece, (((0,), (0,)), ((), ())), preferred_element_type=jnp.float32
            )
    diag[0:128] = term[:128, :128]
    diag[128:256] = term[:128, 128:]
    diag[256:384] = term[128:, 128:]
    for hop, out in enumerate((out0, out1, out2, out3)):
        out[...] = full[(y + hop) & 3]


def turn_kernel(in0, in1, in2, in3, out0, out1, out2, out3, full):
    zl = lax.axis_index("zl")
    full[...] = in0[...] + in1[...] + in2[...] + in3[...]
    for hop, out in enumerate((out0, out1, out2, out3)):
        out[...] = full[pl.ds(pl.multiple_of(((zl + hop) & 3) * 64, 64), 64)]


def split_kernel(mask, in0, in1, in2, in3, stay, leave):
    core = lax.axis_index("core")
    own = -mask[lax.axis_index("zl")].astype(jnp.float32)
    column = (in0[...] + in1[...] + in2[...] + in3[...]) * own
    low = jnp.concatenate([column[0:32, 0:128], column[0:32, 128:256]])
    high = jnp.concatenate([column[32:64, 0:128], column[32:64, 128:256]])
    stay[...] = jnp.where(core == 0, low, high)
    leave[...] = jnp.where(core == 0, high, low)


def finish_kernel(total, stay, swapped, inv_one, inv_two, column_one, column_two, diag_one, diag_two):
    first = lax.axis_index("core") == 0
    own, other = total[...], swapped[0:384]
    own_column, other_column = stay[...], swapped[384:448]
    for swap, inv, diag, column in (
        (False, inv_one, diag_one, column_one),
        (True, inv_two, diag_two, column_two),
    ):
        pick = first != swap
        t = jnp.where(pick, own, other)
        c = jnp.where(pick, own_column, other_column).astype(jnp.bfloat16)
        diag[0:128, 0:128] = inv[0:128, 0:128] + t[0:128]
        diag[0:128, 128:256] = inv[0:128, 128:256] + t[128:256]
        diag[128:256, 0:128] = inv[128:256, 0:128] + t[128:256].T
        diag[128:256, 128:256] = inv[128:256, 128:256] + t[256:384]
        column[:, 0:128] = c[0:32]
        column[:, 128:256] = c[32:64]


def call(kernel, outs, args, scratch=(), scalars=0):
    many = isinstance(outs, list)
    return pl.pallas_call(
        kernel,
        out_shape=outs,
        in_specs=[SMEM] * scalars + [VMEM] * (len(args) - scalars),
        out_specs=[VMEM] * len(outs) if many else VMEM,
        scratch_shapes=list(scratch),
        compiler_params=PARAMS,
    )(*args)


def per_device(
    inverse_pool, factor_one, factor_two, diag_inv_one, diag_inv_two, struct_one, struct_two
):
    row_count, width = factor_one.shape
    f32 = jnp.float32
    core = lax.axis_index("core")
    first = core == 0
    struct = jnp.where(first, struct_one, struct_two)
    mask = lax.dynamic_slice_in_dim(struct, lax.axis_index(("x", "zh")) * 4, 4)
    sibling_pool = lax.ppermute(inverse_pool, "core", SWAP)

    both = jnp.broadcast_to(
        jnp.stack([factor_one, factor_two])[None], (4, 2, row_count, width)
    ).reshape(8, row_count, width)
    rows = exchange(both, ("zl", "core")).reshape(4, 2 * row_count, width)
    rows = rows * mask.astype(jnp.bfloat16)[:, None, None]
    rows = lax.optimization_barrier(rows)
    turned = lax.ppermute(rows, AXES, TURN)
    around = lax.all_gather(rows.reshape(256, width), "y")
    turned, around = lax.optimization_barrier((turned, around))
    strip = gather(turned, "x", 4)

    quarter = jax.ShapeDtypeStruct((256, width), f32)
    diag, *parts = call(
        multiply_kernel,
        [jax.ShapeDtypeStruct((384, 128), f32)] + [quarter] * 4,
        (inverse_pool, sibling_pool, strip, around),
        [pltpu.VMEM((1024, width), jnp.bfloat16), pltpu.VMEM((4, 256, width), f32)],
    )
    shard = jnp.sum(exchange(diag.reshape(16, 24, 128), ("x", "y")), axis=0)
    parts = rotate(parts, "y")
    shard = jnp.sum(gather(shard, ("zh", "zl"), 16), axis=0)
    parts = call(
        turn_kernel,
        [jax.ShapeDtypeStruct((2 * row_count, width), f32)] * 4,
        parts,
        [pltpu.VMEM((256, width), f32)],
    )
    parts = rotate(parts, "zl")
    half = jax.ShapeDtypeStruct((2 * row_count, 128), f32)
    stay, leave = call(split_kernel, [half, half], (mask, *parts), scalars=1)
    total = gather(shard, ("x", "y"), 16).reshape(384, 128)
    swapped = lax.ppermute(jnp.concatenate([total, leave]), "core", SWAP)
    wide = jax.ShapeDtypeStruct((row_count, width), jnp.bfloat16)
    square = jax.ShapeDtypeStruct((width, width), f32)
    return tuple(
        call(
            finish_kernel,
            [wide, wide, square, square],
            (total, stay, swapped, diag_inv_one, diag_inv_two),
        )
    )


def solution(mesh):
    fine = Mesh(mesh.devices.reshape(SIZES), AXES)
    rows = P(AXES, None)
    in_specs = (P(("x", "zh"), ("zl", "y", "core")), rows, rows, P(), P(), P(), P())
    out_specs = (rows, rows, P(), P())
    return jax.shard_map(
        per_device, mesh=fine, in_specs=in_specs, out_specs=out_specs, check_vma=False
    )
```

```python
import jax
import jax.numpy as jnp
from jax import lax
from jax.experimental import pallas as pl
from jax.experimental.pallas import tpu as pltpu
from jax.sharding import Mesh, PartitionSpec as P

AXES = ("x", "zh", "zl", "y", "core")
SIZES = (4, 4, 4, 4, 2)
SWAP = [(0, 1), (1, 0)]
VMEM = pl.BlockSpec(memory_space=pltpu.VMEM)
ANY = pl.BlockSpec(memory_space=pl.ANY)
SMEM = pl.BlockSpec(memory_space=pltpu.SMEM)
PARAMS = pltpu.CompilerParams(vmem_limit_bytes=32 * 1024 * 1024)


def exchange(parts, axes):
    return lax.all_to_all(parts, axes, 0, 0)


def gather(block, axes, count):
    return exchange(jnp.broadcast_to(block[None], (count, *block.shape)), axes)


def rotate(parts, axis):
    return [parts[0]] + [
        lax.ppermute(parts[s], axis, [(i, (i + s) % 4) for i in range(4)]) for s in (1, 2, 3)
    ]


def device_id(x, zh, zl, y, core):
    return (((x * 4 + zh) * 4 + zl) * 4 + y) * 2 + core


def turn_source(x, zh, zl, y):
    near = (1, 2, 3, 0) if zl < 2 else (2, 3, 0, 1)
    return zl, y, near[(zh - y) % 4], (y + 2 + x - zl) % 4


TURN = [
    (device_id(*turn_source(a, b, c, d), k), device_id(a, b, c, d, k))
    for a in range(4)
    for b in range(4)
    for c in range(4)
    for d in range(4)
    for k in range(2)
]


def spread_kernel(one, two, out, sems):
    copies = [
        pltpu.make_async_copy(source, out.at[2 * z + k], sems.at[2 * z + k])
        for z in range(4)
        for k, source in enumerate((one, two))
    ]
    for copy in copies:
        copy.start()
    for copy in copies:
        copy.wait()


def multiply_kernel(pool, sibling, strip, rows, diag, out0, out1, out2, out3, rhs, full):
    core, y = lax.axis_index("core"), lax.axis_index("y")
    shift = lax.axis_index("zl") - y + 2
    depth = rhs.shape[0] // 2
    for side, which in ((0, core), (1, 1 - core)):
        for h in range(2):
            for j in range(4):
                start = side * depth + h * 256 + j * 64
                rhs[start : start + 64] = strip[(j + shift) & 3, 2 * which + h]
    for z in range(4):
        take = slice(z * 256, (z + 1) * 256)
        block = jnp.dot(
            pool[take], rhs[:depth], preferred_element_type=jnp.float32
        ) + jnp.dot(sibling[take], rhs[depth:], preferred_element_type=jnp.float32)
        for j in range(4):
            full[j, z * 64 : (z + 1) * 64] = block[j * 64 : (j + 1) * 64]
    terms = jnp.zeros((256, 768), jnp.float32)
    for j in range(4):
        pieces, rest = [], full[j]
        for _ in range(3):
            pieces.append(rest.astype(jnp.bfloat16))
            rest = rest - pieces[-1].astype(jnp.float32)
        terms = terms + lax.dot_general(
            rows[j],
            jnp.concatenate(pieces, axis=1),
            (((0,), (0,)), ((), ())),
            preferred_element_type=jnp.float32,
        )
    term = terms[:, :256] + terms[:, 256:512] + terms[:, 512:]
    diag[0:128] = term[:128, :128]
    diag[128:256] = term[:128, 128:]
    diag[256:384] = term[128:, 128:]
    for hop, out in enumerate((out0, out1, out2, out3)):
        out[...] = full[(y + hop) & 3]


def turn_kernel(in0, in1, in2, in3, out0, out1, out2, out3, full):
    zl = lax.axis_index("zl")
    full[...] = in0[...] + in1[...] + in2[...] + in3[...]
    for hop, out in enumerate((out0, out1, out2, out3)):
        out[...] = full[pl.ds(pl.multiple_of(((zl + hop) & 3) * 64, 64), 64)]


def split_kernel(mask, in0, in1, in2, in3, stay, leave):
    core = lax.axis_index("core")
    own = -mask[lax.axis_index("zl")].astype(jnp.float32)
    column = (in0[...] + in1[...] + in2[...] + in3[...]) * own
    low = jnp.concatenate([column[0:32, 0:128], column[0:32, 128:256]])
    high = jnp.concatenate([column[32:64, 0:128], column[32:64, 128:256]])
    stay[...] = jnp.where(core == 0, low, high)
    leave[...] = jnp.where(core == 0, high, low)


def finish_kernel(total, stay, swapped, inv_one, inv_two, column_one, column_two, diag_one, diag_two):
    first = lax.axis_index("core") == 0
    own, other = total[...], swapped[0:384]
    own_column, other_column = stay[...], swapped[384:448]
    for swap, inv, diag, column in (
        (False, inv_one, diag_one, column_one),
        (True, inv_two, diag_two, column_two),
    ):
        pick = first != swap
        t = jnp.where(pick, own, other)
        c = jnp.where(pick, own_column, other_column).astype(jnp.bfloat16)
        diag[0:128, 0:128] = inv[0:128, 0:128] + t[0:128]
        diag[0:128, 128:256] = inv[0:128, 128:256] + t[128:256]
        diag[128:256, 0:128] = inv[128:256, 0:128] + t[128:256].T
        diag[128:256, 128:256] = inv[128:256, 128:256] + t[256:384]
        column[:, 0:128] = c[0:32]
        column[:, 128:256] = c[32:64]


def call(kernel, outs, args, scratch=(), scalars=0):
    many = isinstance(outs, list)
    return pl.pallas_call(
        kernel,
        out_shape=outs,
        in_specs=[SMEM] * scalars + [VMEM] * (len(args) - scalars),
        out_specs=[VMEM] * len(outs) if many else VMEM,
        scratch_shapes=list(scratch),
        compiler_params=PARAMS,
    )(*args)


def per_device(
    inverse_pool, factor_one, factor_two, diag_inv_one, diag_inv_two, struct_one, struct_two
):
    row_count, width = factor_one.shape
    f32 = jnp.float32
    core = lax.axis_index("core")
    first = core == 0
    struct = jnp.where(first, struct_one, struct_two)
    mask = lax.dynamic_slice_in_dim(struct, lax.axis_index(("x", "zh")) * 4, 4)
    sibling_pool = lax.ppermute(inverse_pool, "core", SWAP)

    both = pl.pallas_call(
        spread_kernel,
        out_shape=jax.ShapeDtypeStruct((8, row_count, width), factor_one.dtype),
        in_specs=[ANY, ANY],
        out_specs=ANY,
        scratch_shapes=[pltpu.SemaphoreType.DMA((8,))],
    )(factor_one, factor_two)
    rows = exchange(both, ("zl", "core")).reshape(4, 2 * row_count, width)
    rows = rows * mask.astype(jnp.bfloat16)[:, None, None]
    rows = lax.optimization_barrier(rows)
    turned = lax.ppermute(rows, AXES, TURN)
    around = lax.all_gather(rows.reshape(256, width), "y")
    turned, around = lax.optimization_barrier((turned, around))
    strip = gather(turned, "x", 4)

    quarter = jax.ShapeDtypeStruct((256, width), f32)
    diag, *parts = call(
        multiply_kernel,
        [jax.ShapeDtypeStruct((384, 128), f32)] + [quarter] * 4,
        (inverse_pool, sibling_pool, strip, around),
        [pltpu.VMEM((1024, width), jnp.bfloat16), pltpu.VMEM((4, 256, width), f32)],
    )
    shard = jnp.sum(exchange(diag.reshape(16, 24, 128), ("x", "y")), axis=0)
    parts = rotate(parts, "y")
    shard = jnp.sum(gather(shard, ("zh", "zl"), 16), axis=0)
    parts = call(
        turn_kernel,
        [jax.ShapeDtypeStruct((2 * row_count, width), f32)] * 4,
        parts,
        [pltpu.VMEM((256, width), f32)],
    )
    parts = rotate(parts, "zl")
    half = jax.ShapeDtypeStruct((2 * row_count, 128), f32)
    stay, leave = call(split_kernel, [half, half], (mask, *parts), scalars=1)
    total = gather(shard, ("x", "y"), 16).reshape(384, 128)
    swapped = lax.ppermute(jnp.concatenate([total, leave]), "core", SWAP)
    wide = jax.ShapeDtypeStruct((row_count, width), jnp.bfloat16)
    square = jax.ShapeDtypeStruct((width, width), f32)
    return tuple(
        call(
            finish_kernel,
            [wide, wide, square, square],
            (total, stay, swapped, diag_inv_one, diag_inv_two),
        )
    )


def solution(mesh):
    fine = Mesh(mesh.devices.reshape(SIZES), AXES)
    rows = P(AXES, None)
    in_specs = (P(("x", "zh"), ("zl", "y", "core")), rows, rows, P(), P(), P(), P())
    out_specs = (rows, rows, P(), P())
    return jax.shard_map(
        per_device, mesh=fine, in_specs=in_specs, out_specs=out_specs, check_vma=False
    )
```

```python
import jax
import jax.numpy as jnp
from jax import lax
from jax.experimental import pallas as pl
from jax.experimental.pallas import tpu as pltpu
from jax.sharding import Mesh, PartitionSpec as P

AXES = ("x", "zh", "zl", "y", "core")
SIZES = (4, 4, 4, 4, 2)
SWAP = [(0, 1), (1, 0)]
VMEM = pl.BlockSpec(memory_space=pltpu.VMEM)
SMEM = pl.BlockSpec(memory_space=pltpu.SMEM)
PARAMS = pltpu.CompilerParams(vmem_limit_bytes=32 * 1024 * 1024)


def exchange(parts, axes):
    return lax.all_to_all(parts, axes, 0, 0)


def gather(block, axes, count):
    return exchange(jnp.broadcast_to(block[None], (count, *block.shape)), axes)


def rotate(parts, axis):
    return [parts[0]] + [
        lax.ppermute(parts[s], axis, [(i, (i + s) % 4) for i in range(4)]) for s in (1, 2, 3)
    ]


def device_id(x, zh, zl, y, core):
    return (((x * 4 + zh) * 4 + zl) * 4 + y) * 2 + core


def turn_source(x, zh, zl, y):
    near = (1, 2, 3, 0) if zl < 2 else (2, 3, 0, 1)
    return zl, y, near[(zh - y) % 4], (y + 2 + x - zl) % 4


TURN = [
    (device_id(*turn_source(a, b, c, d), k), device_id(a, b, c, d, k))
    for a in range(4)
    for b in range(4)
    for c in range(4)
    for d in range(4)
    for k in range(2)
]


def multiply_kernel(pool, sibling, strip, rows, diag, out0, out1, out2, out3, rhs, full):
    core, y = lax.axis_index("core"), lax.axis_index("y")
    shift = lax.axis_index("zl") - y + 2
    depth = rhs.shape[0] // 2
    for side, which in ((0, core), (1, 1 - core)):
        for h in range(2):
            for j in range(4):
                start = side * depth + h * 256 + j * 64
                rhs[start : start + 64] = strip[(j + shift) & 3, 2 * which + h]
    for z in range(4):
        take = slice(z * 256, (z + 1) * 256)
        block = jnp.dot(
            pool[take], rhs[:depth], preferred_element_type=jnp.float32
        ) + jnp.dot(sibling[take], rhs[depth:], preferred_element_type=jnp.float32)
        for j in range(4):
            full[j, z * 64 : (z + 1) * 64] = block[j * 64 : (j + 1) * 64]
    term = jnp.zeros((256, 256), jnp.float32)
    for j in range(4):
        left, rest = rows[j], full[j]
        for _ in range(3):
            piece = rest.astype(jnp.bfloat16)
            rest = rest - piece.astype(jnp.float32)
            term = term + lax.dot_general(
                left, piece, (((0,), (0,)), ((), ())), preferred_element_type=jnp.float32
            )
    diag[0:128] = term[:128, :128]
    diag[128:256] = term[:128, 128:]
    diag[256:384] = term[128:, 128:]
    for hop, out in enumerate((out0, out1, out2, out3)):
        out[...] = full[(y + hop) & 3]


def turn_kernel(in0, in1, in2, in3, out0, out1, out2, out3, full):
    zl = lax.axis_index("zl")
    full[...] = in0[...] + in1[...] + in2[...] + in3[...]
    for hop, out in enumerate((out0, out1, out2, out3)):
        out[...] = full[pl.ds(pl.multiple_of(((zl + hop) & 3) * 64, 64), 64)]


def split_kernel(mask, in0, in1, in2, in3, stay, leave):
    core = lax.axis_index("core")
    own = -mask[lax.axis_index("zl")].astype(jnp.float32)
    column = (in0[...] + in1[...] + in2[...] + in3[...]) * own
    low = jnp.concatenate([column[0:32, 0:128], column[0:32, 128:256]])
    high = jnp.concatenate([column[32:64, 0:128], column[32:64, 128:256]])
    stay[...] = jnp.where(core == 0, low, high)
    leave[...] = jnp.where(core == 0, high, low)


def finish_kernel(finals, stay, inv_one, inv_two, column_one, column_two, diag_one, diag_two):
    first = lax.axis_index("core") == 0
    for k, inv, diag, column in (
        (0, inv_one, diag_one, column_one),
        (1, inv_two, diag_two, column_two),
    ):
        t = finals[k, 0:384]
        c = jnp.where(first == (k == 0), stay[...], finals[k, 384:448]).astype(jnp.bfloat16)
        diag[0:128, 0:128] = inv[0:128, 0:128] + t[0:128]
        diag[0:128, 128:256] = inv[0:128, 128:256] + t[128:256]
        diag[128:256, 0:128] = inv[128:256, 0:128] + t[128:256].T
        diag[128:256, 128:256] = inv[128:256, 128:256] + t[256:384]
        column[:, 0:128] = c[0:32]
        column[:, 128:256] = c[32:64]


def call(kernel, outs, args, scratch=(), scalars=0):
    many = isinstance(outs, list)
    return pl.pallas_call(
        kernel,
        out_shape=outs,
        in_specs=[SMEM] * scalars + [VMEM] * (len(args) - scalars),
        out_specs=[VMEM] * len(outs) if many else VMEM,
        scratch_shapes=list(scratch),
        compiler_params=PARAMS,
    )(*args)


def per_device(
    inverse_pool, factor_one, factor_two, diag_inv_one, diag_inv_two, struct_one, struct_two
):
    row_count, width = factor_one.shape
    f32 = jnp.float32
    core = lax.axis_index("core")
    first = core == 0
    struct = jnp.where(first, struct_one, struct_two)
    mask = lax.dynamic_slice_in_dim(struct, lax.axis_index(("x", "zh")) * 4, 4)
    sibling_pool = lax.ppermute(inverse_pool, "core", SWAP)

    both = jnp.broadcast_to(
        jnp.stack([factor_one, factor_two])[None], (4, 2, row_count, width)
    ).reshape(8, row_count, width)
    rows = exchange(both, ("zl", "core")).reshape(4, 2 * row_count, width)
    rows = rows * mask.astype(jnp.bfloat16)[:, None, None]
    rows = lax.optimization_barrier(rows)
    turned = lax.ppermute(rows, AXES, TURN)
    around = lax.all_gather(rows.reshape(256, width), "y")
    turned, around = lax.optimization_barrier((turned, around))
    strip = gather(turned, "x", 4)

    quarter = jax.ShapeDtypeStruct((256, width), f32)
    diag, *parts = call(
        multiply_kernel,
        [jax.ShapeDtypeStruct((384, 128), f32)] + [quarter] * 4,
        (inverse_pool, sibling_pool, strip, around),
        [pltpu.VMEM((1024, width), jnp.bfloat16), pltpu.VMEM((4, 256, width), f32)],
    )
    shard = jnp.sum(exchange(diag.reshape(16, 24, 128), ("x", "y")), axis=0)
    parts = rotate(parts, "y")
    shard = jnp.sum(gather(shard, ("zh", "zl"), 16), axis=0)
    parts = call(
        turn_kernel,
        [jax.ShapeDtypeStruct((2 * row_count, width), f32)] * 4,
        parts,
        [pltpu.VMEM((256, width), f32)],
    )
    parts = rotate(parts, "zl")
    half = jax.ShapeDtypeStruct((2 * row_count, 128), f32)
    stay, leave = call(split_kernel, [half, half], (mask, *parts), scalars=1)
    total = gather(shard, ("x", "y"), 16).reshape(384, 128)
    finals = lax.all_gather(jnp.concatenate([total, leave]), "core")
    wide = jax.ShapeDtypeStruct((row_count, width), jnp.bfloat16)
    square = jax.ShapeDtypeStruct((width, width), f32)
    return tuple(
        call(
            finish_kernel,
            [wide, wide, square, square],
            (finals, stay, diag_inv_one, diag_inv_two),
        )
    )


def solution(mesh):
    fine = Mesh(mesh.devices.reshape(SIZES), AXES)
    rows = P(AXES, None)
    in_specs = (P(("x", "zh"), ("zl", "y", "core")), rows, rows, P(), P(), P(), P())
    out_specs = (rows, rows, P(), P())
    return jax.shard_map(
        per_device, mesh=fine, in_specs=in_specs, out_specs=out_specs, check_vma=False
    )
```

```python
import jax
import jax.numpy as jnp
from jax import lax
from jax.experimental import pallas as pl
from jax.experimental.pallas import tpu as pltpu
from jax.sharding import Mesh, PartitionSpec as P

AXES = ("x", "zh", "zl", "yh", "yl", "core")
SIZES = (4, 4, 4, 2, 2, 2)
Y = ("yh", "yl")
SWAP = [(0, 1), (1, 0)]
VMEM = pl.BlockSpec(memory_space=pltpu.VMEM)
SMEM = pl.BlockSpec(memory_space=pltpu.SMEM)
PARAMS = pltpu.CompilerParams(vmem_limit_bytes=32 * 1024 * 1024)


def y_index():
    return lax.axis_index("yh") * 2 + lax.axis_index("yl")


def exchange(parts, axes):
    return lax.all_to_all(parts, axes, 0, 0)


def gather(block, axes, count):
    return exchange(jnp.broadcast_to(block[None], (count, *block.shape)), axes)


def rotate(parts, axis):
    return [parts[0]] + [
        lax.ppermute(parts[s], axis, [(i, (i + s) % 4) for i in range(4)]) for s in (1, 2, 3)
    ]


def device_id(x, zh, zl, y, core):
    return (((x * 4 + zh) * 4 + zl) * 4 + y) * 2 + core


def turn_source(x, zh, zl, y):
    near = (1, 2, 3, 0) if zl < 2 else (2, 3, 0, 1)
    return zl, y, near[(zh - y) % 4], (y + 2 + x - zl) % 4


TURN = [
    (device_id(*turn_source(a, b, c, d), k), device_id(a, b, c, d, k))
    for a in range(4)
    for b in range(4)
    for c in range(4)
    for d in range(4)
    for k in range(2)
]


def multiply_kernel(pool, sibling, strip, rows, diag, out0, out1, out2, out3, rhs, full):
    core, y = lax.axis_index("core"), y_index()
    shift = lax.axis_index("zl") - y + 2
    depth = rhs.shape[0] // 2
    for side, which in ((0, core), (1, 1 - core)):
        for h in range(2):
            for j in range(4):
                start = side * depth + h * 256 + j * 64
                rhs[start : start + 64] = strip[(j + shift) & 3, 2 * which + h]
    for z in range(4):
        take = slice(z * 256, (z + 1) * 256)
        block = jnp.dot(
            pool[take], rhs[:depth], preferred_element_type=jnp.float32
        ) + jnp.dot(sibling[take], rhs[depth:], preferred_element_type=jnp.float32)
        for j in range(4):
            full[j, z * 64 : (z + 1) * 64] = block[j * 64 : (j + 1) * 64]
    term = jnp.zeros((256, 256), jnp.float32)
    for j in range(4):
        left, rest = rows[(j & 1) * 2 + (j >> 1)], full[j]
        for _ in range(3):
            piece = rest.astype(jnp.bfloat16)
            rest = rest - piece.astype(jnp.float32)
            term = term + lax.dot_general(
                left, piece, (((0,), (0,)), ((), ())), preferred_element_type=jnp.float32
            )
    diag[0:128] = term[:128, :128]
    diag[128:256] = term[:128, 128:]
    diag[256:384] = term[128:, 128:]
    for hop, out in enumerate((out0, out1, out2, out3)):
        out[...] = full[(y + hop) & 3]


def turn_kernel(in0, in1, in2, in3, out0, out1, out2, out3, full):
    zl = lax.axis_index("zl")
    full[...] = in0[...] + in1[...] + in2[...] + in3[...]
    for hop, out in enumerate((out0, out1, out2, out3)):
        out[...] = full[pl.ds(pl.multiple_of(((zl + hop) & 3) * 64, 64), 64)]


def split_kernel(mask, in0, in1, in2, in3, stay, leave):
    core = lax.axis_index("core")
    own = -mask[lax.axis_index("zl")].astype(jnp.float32)
    column = (in0[...] + in1[...] + in2[...] + in3[...]) * own
    low = jnp.concatenate([column[0:32, 0:128], column[0:32, 128:256]])
    high = jnp.concatenate([column[32:64, 0:128], column[32:64, 128:256]])
    stay[...] = jnp.where(core == 0, low, high)
    leave[...] = jnp.where(core == 0, high, low)


def finish_kernel(finals, stay, inv_one, inv_two, column_one, column_two, diag_one, diag_two):
    first = lax.axis_index("core") == 0
    for k, inv, diag, column in (
        (0, inv_one, diag_one, column_one),
        (1, inv_two, diag_two, column_two),
    ):
        t = finals[k, 0:384]
        c = jnp.where(first == (k == 0), stay[...], finals[k, 384:448]).astype(jnp.bfloat16)
        diag[0:128, 0:128] = inv[0:128, 0:128] + t[0:128]
        diag[0:128, 128:256] = inv[0:128, 128:256] + t[128:256]
        diag[128:256, 0:128] = inv[128:256, 0:128] + t[128:256].T
        diag[128:256, 128:256] = inv[128:256, 128:256] + t[256:384]
        column[:, 0:128] = c[0:32]
        column[:, 128:256] = c[32:64]


def call(kernel, outs, args, scratch=(), scalars=0):
    many = isinstance(outs, list)
    return pl.pallas_call(
        kernel,
        out_shape=outs,
        in_specs=[SMEM] * scalars + [VMEM] * (len(args) - scalars),
        out_specs=[VMEM] * len(outs) if many else VMEM,
        scratch_shapes=list(scratch),
        compiler_params=PARAMS,
    )(*args)


def per_device(
    inverse_pool, factor_one, factor_two, diag_inv_one, diag_inv_two, struct_one, struct_two
):
    row_count, width = factor_one.shape
    f32 = jnp.float32
    core = lax.axis_index("core")
    first = core == 0
    struct = jnp.where(first, struct_one, struct_two)
    mask = lax.dynamic_slice_in_dim(struct, lax.axis_index(("x", "zh")) * 4, 4)
    sibling_pool = lax.ppermute(inverse_pool, "core", SWAP)

    both = jnp.broadcast_to(
        jnp.stack([factor_one, factor_two])[None], (4, 2, row_count, width)
    ).reshape(8, row_count, width)
    rows = exchange(both, ("zl", "core")).reshape(4, 2 * row_count, width)
    rows = rows * mask.astype(jnp.bfloat16)[:, None, None]
    rows = lax.optimization_barrier(rows)
    turned = lax.ppermute(rows, AXES, TURN)
    around = lax.all_gather(rows.reshape(256, width), "yh")
    around = lax.all_gather(around, "yl").reshape(4, 256, width)
    turned, around = lax.optimization_barrier((turned, around))
    strip = gather(turned, "x", 4)

    quarter = jax.ShapeDtypeStruct((256, width), f32)
    diag, *parts = call(
        multiply_kernel,
        [jax.ShapeDtypeStruct((384, 128), f32)] + [quarter] * 4,
        (inverse_pool, sibling_pool, strip, around),
        [pltpu.VMEM((1024, width), jnp.bfloat16), pltpu.VMEM((4, 256, width), f32)],
    )
    shard = jnp.sum(exchange(diag.reshape(16, 24, 128), ("x", *Y)), axis=0)
    parts = rotate(parts, Y)
    shard = jnp.sum(gather(shard, ("zh", "zl"), 16), axis=0)
    parts = call(
        turn_kernel,
        [jax.ShapeDtypeStruct((2 * row_count, width), f32)] * 4,
        parts,
        [pltpu.VMEM((256, width), f32)],
    )
    parts = rotate(parts, "zl")
    half = jax.ShapeDtypeStruct((2 * row_count, 128), f32)
    stay, leave = call(split_kernel, [half, half], (mask, *parts), scalars=1)
    total = gather(shard, ("x", *Y), 16).reshape(384, 128)
    finals = lax.all_gather(jnp.concatenate([total, leave]), "core")
    wide = jax.ShapeDtypeStruct((row_count, width), jnp.bfloat16)
    square = jax.ShapeDtypeStruct((width, width), f32)
    return tuple(
        call(
            finish_kernel,
            [wide, wide, square, square],
            (finals, stay, diag_inv_one, diag_inv_two),
        )
    )


def solution(mesh):
    fine = Mesh(mesh.devices.reshape(SIZES), AXES)
    rows = P(AXES, None)
    in_specs = (P(("x", "zh"), ("zl", *Y, "core")), rows, rows, P(), P(), P(), P())
    out_specs = (rows, rows, P(), P())
    return jax.shard_map(
        per_device, mesh=fine, in_specs=in_specs, out_specs=out_specs, check_vma=False
    )
```

```python
import jax
import jax.numpy as jnp
from jax import lax
from jax.experimental import pallas as pl
from jax.experimental.pallas import tpu as pltpu
from jax.sharding import Mesh, PartitionSpec as P

AXES = ("x", "zh", "zl", "y", "core")
SIZES = (4, 4, 4, 4, 2)
SWAP = [(0, 1), (1, 0)]
VMEM = pl.BlockSpec(memory_space=pltpu.VMEM)
SMEM = pl.BlockSpec(memory_space=pltpu.SMEM)
PARAMS = pltpu.CompilerParams(vmem_limit_bytes=32 * 1024 * 1024)


def exchange(parts, axes):
    return lax.all_to_all(parts, axes, 0, 0)


def gather(block, axes, count):
    return exchange(jnp.broadcast_to(block[None], (count, *block.shape)), axes)


def rotate(parts, axis):
    return [parts[0]] + [
        lax.ppermute(parts[s], axis, [(i, i ^ s) for i in range(4)]) for s in (1, 2, 3)
    ]


def device_id(x, zh, zl, y, core):
    return (((x * 4 + zh) * 4 + zl) * 4 + y) * 2 + core


def turn_source(x, zh, zl, y):
    near = (1, 2, 3, 0) if zl < 2 else (2, 3, 0, 1)
    return zl, y, near[(zh - y) % 4], (y + 2 + x - zl) % 4


TURN = [
    (device_id(*turn_source(a, b, c, d), k), device_id(a, b, c, d, k))
    for a in range(4)
    for b in range(4)
    for c in range(4)
    for d in range(4)
    for k in range(2)
]


def multiply_kernel(pool, sibling, strip, rows, diag, out0, out1, out2, out3, rhs, full):
    core, y = lax.axis_index("core"), lax.axis_index("y")
    shift = lax.axis_index("zl") - y + 2
    depth = rhs.shape[0] // 2
    for side, which in ((0, core), (1, 1 - core)):
        for h in range(2):
            for j in range(4):
                start = side * depth + h * 256 + j * 64
                rhs[start : start + 64] = strip[(j + shift) & 3, 2 * which + h]
    for z in range(4):
        take = slice(z * 256, (z + 1) * 256)
        block = jnp.dot(
            pool[take], rhs[:depth], preferred_element_type=jnp.float32
        ) + jnp.dot(sibling[take], rhs[depth:], preferred_element_type=jnp.float32)
        for j in range(4):
            full[j, z * 64 : (z + 1) * 64] = block[j * 64 : (j + 1) * 64]
    term = jnp.zeros((256, 256), jnp.float32)
    for j in range(4):
        left, rest = rows[j], full[j]
        for _ in range(3):
            piece = rest.astype(jnp.bfloat16)
            rest = rest - piece.astype(jnp.float32)
            term = term + lax.dot_general(
                left, piece, (((0,), (0,)), ((), ())), preferred_element_type=jnp.float32
            )
    diag[0:128] = term[:128, :128]
    diag[128:256] = term[:128, 128:]
    diag[256:384] = term[128:, 128:]
    for hop, out in enumerate((out0, out1, out2, out3)):
        out[...] = full[y ^ hop]


def turn_kernel(in0, in1, in2, in3, out0, out1, out2, out3, full):
    zl = lax.axis_index("zl")
    full[...] = in0[...] + in1[...] + in2[...] + in3[...]
    for hop, out in enumerate((out0, out1, out2, out3)):
        out[...] = full[pl.ds(pl.multiple_of((zl ^ hop) * 64, 64), 64)]


def split_kernel(mask, in0, in1, in2, in3, stay, leave):
    core = lax.axis_index("core")
    own = -mask[lax.axis_index("zl")].astype(jnp.float32)
    column = (in0[...] + in1[...] + in2[...] + in3[...]) * own
    low = jnp.concatenate([column[0:32, 0:128], column[0:32, 128:256]])
    high = jnp.concatenate([column[32:64, 0:128], column[32:64, 128:256]])
    stay[...] = jnp.where(core == 0, low, high)
    leave[...] = jnp.where(core == 0, high, low)


def finish_kernel(finals, stay, inv_one, inv_two, column_one, column_two, diag_one, diag_two):
    first = lax.axis_index("core") == 0
    for k, inv, diag, column in (
        (0, inv_one, diag_one, column_one),
        (1, inv_two, diag_two, column_two),
    ):
        t = finals[k, 0:384]
        c = jnp.where(first == (k == 0), stay[...], finals[k, 384:448]).astype(jnp.bfloat16)
        diag[0:128, 0:128] = inv[0:128, 0:128] + t[0:128]
        diag[0:128, 128:256] = inv[0:128, 128:256] + t[128:256]
        diag[128:256, 0:128] = inv[128:256, 0:128] + t[128:256].T
        diag[128:256, 128:256] = inv[128:256, 128:256] + t[256:384]
        column[:, 0:128] = c[0:32]
        column[:, 128:256] = c[32:64]


def call(kernel, outs, args, scratch=(), scalars=0):
    many = isinstance(outs, list)
    return pl.pallas_call(
        kernel,
        out_shape=outs,
        in_specs=[SMEM] * scalars + [VMEM] * (len(args) - scalars),
        out_specs=[VMEM] * len(outs) if many else VMEM,
        scratch_shapes=list(scratch),
        compiler_params=PARAMS,
    )(*args)


def per_device(
    inverse_pool, factor_one, factor_two, diag_inv_one, diag_inv_two, struct_one, struct_two
):
    row_count, width = factor_one.shape
    f32 = jnp.float32
    core = lax.axis_index("core")
    first = core == 0
    struct = jnp.where(first, struct_one, struct_two)
    mask = lax.dynamic_slice_in_dim(struct, lax.axis_index(("x", "zh")) * 4, 4)
    sibling_pool = lax.ppermute(inverse_pool, "core", SWAP)

    both = jnp.broadcast_to(
        jnp.stack([factor_one, factor_two])[None], (4, 2, row_count, width)
    ).reshape(8, row_count, width)
    rows = exchange(both, ("zl", "core")).reshape(4, 2 * row_count, width)
    rows = rows * mask.astype(jnp.bfloat16)[:, None, None]
    rows = lax.optimization_barrier(rows)
    turned = lax.ppermute(rows, AXES, TURN)
    around = lax.all_gather(rows.reshape(256, width), "y")
    turned, around = lax.optimization_barrier((turned, around))
    strip = gather(turned, "x", 4)

    quarter = jax.ShapeDtypeStruct((256, width), f32)
    diag, *parts = call(
        multiply_kernel,
        [jax.ShapeDtypeStruct((384, 128), f32)] + [quarter] * 4,
        (inverse_pool, sibling_pool, strip, around),
        [pltpu.VMEM((1024, width), jnp.bfloat16), pltpu.VMEM((4, 256, width), f32)],
    )
    shard = jnp.sum(exchange(diag.reshape(16, 24, 128), ("x", "y")), axis=0)
    parts = rotate(parts, "y")
    shard = jnp.sum(gather(shard, ("zh", "zl"), 16), axis=0)
    parts = call(
        turn_kernel,
        [jax.ShapeDtypeStruct((2 * row_count, width), f32)] * 4,
        parts,
        [pltpu.VMEM((256, width), f32)],
    )
    parts = rotate(parts, "zl")
    half = jax.ShapeDtypeStruct((2 * row_count, 128), f32)
    stay, leave = call(split_kernel, [half, half], (mask, *parts), scalars=1)
    total = gather(shard, ("x", "y"), 16).reshape(384, 128)
    finals = lax.all_gather(jnp.concatenate([total, leave]), "core")
    wide = jax.ShapeDtypeStruct((row_count, width), jnp.bfloat16)
    square = jax.ShapeDtypeStruct((width, width), f32)
    return tuple(
        call(
            finish_kernel,
            [wide, wide, square, square],
            (finals, stay, diag_inv_one, diag_inv_two),
        )
    )


def solution(mesh):
    fine = Mesh(mesh.devices.reshape(SIZES), AXES)
    rows = P(AXES, None)
    in_specs = (P(("x", "zh"), ("zl", "y", "core")), rows, rows, P(), P(), P(), P())
    out_specs = (rows, rows, P(), P())
    return jax.shard_map(
        per_device, mesh=fine, in_specs=in_specs, out_specs=out_specs, check_vma=False
    )
```

```python
import jax
import jax.numpy as jnp
from jax import lax
from jax.experimental import pallas as pl
from jax.experimental.pallas import tpu as pltpu
from jax.sharding import Mesh, PartitionSpec as P

AXES = ("x", "zh", "zl", "y", "core")
SIZES = (4, 4, 4, 4, 2)
SWAP = [(0, 1), (1, 0)]
VMEM = pl.BlockSpec(memory_space=pltpu.VMEM)
SMEM = pl.BlockSpec(memory_space=pltpu.SMEM)
PARAMS = pltpu.CompilerParams(vmem_limit_bytes=32 * 1024 * 1024)


def exchange(parts, axes):
    return lax.all_to_all(parts, axes, 0, 0)


def gather(block, axes, count):
    return exchange(jnp.broadcast_to(block[None], (count, *block.shape)), axes)


def rotate(parts, axis):
    return [parts[0]] + [
        lax.ppermute(parts[s], axis, [(i, (i + s) % 4) for i in range(4)]) for s in (1, 2, 3)
    ]


def device_id(x, zh, zl, y, core):
    return (((x * 4 + zh) * 4 + zl) * 4 + y) * 2 + core


def turn_source(x, zh, zl, y):
    near = (1, 2, 3, 0) if zl < 2 else (2, 3, 0, 1)
    return zl, y, near[(zh - y) % 4], (y + 2 + x - zl) % 4


TURN = [
    (device_id(*turn_source(a, b, c, d), k), device_id(a, b, c, d, k))
    for a in range(4)
    for b in range(4)
    for c in range(4)
    for d in range(4)
    for k in range(2)
]


def multiply_kernel(pool, sibling, strip, rows, diag, out0, out1, out2, out3, rhs, full):
    core, y = lax.axis_index("core"), lax.axis_index("y")
    shift = lax.axis_index("zl") - y + 2
    depth = rhs.shape[0] // 2
    for side, which in ((0, core), (1, 1 - core)):
        for h in range(2):
            for j in range(4):
                start = side * depth + h * 256 + j * 64
                rhs[start : start + 64] = strip[(j + shift) & 3, 2 * which + h]
    for z in range(4):
        take = slice(z * 256, (z + 1) * 256)
        block = jnp.dot(
            pool[take], rhs[:depth], preferred_element_type=jnp.float32
        ) + jnp.dot(sibling[take], rhs[depth:], preferred_element_type=jnp.float32)
        for j in range(4):
            full[j, z * 64 : (z + 1) * 64] = block[j * 64 : (j + 1) * 64]
    term = jnp.zeros((256, 256), jnp.float32)
    for j in range(4):
        left, rest = rows[j], full[j]
        for _ in range(3):
            piece = rest.astype(jnp.bfloat16)
            rest = rest - piece.astype(jnp.float32)
            term = term + lax.dot_general(
                left, piece, (((0,), (0,)), ((), ())), preferred_element_type=jnp.float32
            )
    diag[0:128] = term[:128, :128]
    diag[128:256] = term[:128, 128:]
    diag[256:384] = term[128:, 128:]
    for hop, out in enumerate((out0, out1, out2, out3)):
        out[...] = full[(y + hop) & 3]


def turn_kernel(in0, in1, in2, in3, out0, out1, out2, out3, full):
    zl = lax.axis_index("zl")
    full[...] = in0[...] + in1[...] + in2[...] + in3[...]
    for hop, out in enumerate((out0, out1, out2, out3)):
        out[...] = full[pl.ds(pl.multiple_of((zl ^ hop) * 64, 64), 64)]


def split_kernel(mask, in0, in1, in2, in3, stay, leave):
    core = lax.axis_index("core")
    own = -mask[lax.axis_index("zl")].astype(jnp.float32)
    column = (in0[...] + in1[...] + in2[...] + in3[...]) * own
    low = jnp.concatenate([column[0:32, 0:128], column[0:32, 128:256]])
    high = jnp.concatenate([column[32:64, 0:128], column[32:64, 128:256]])
    stay[...] = jnp.where(core == 0, low, high)
    leave[...] = jnp.where(core == 0, high, low)


def finish_kernel(finals, stay, inv_one, inv_two, column_one, column_two, diag_one, diag_two):
    first = lax.axis_index("core") == 0
    for k, inv, diag, column in (
        (0, inv_one, diag_one, column_one),
        (1, inv_two, diag_two, column_two),
    ):
        t = finals[k, 0:384]
        c = jnp.where(first == (k == 0), stay[...], finals[k, 384:448]).astype(jnp.bfloat16)
        diag[0:128, 0:128] = inv[0:128, 0:128] + t[0:128]
        diag[0:128, 128:256] = inv[0:128, 128:256] + t[128:256]
        diag[128:256, 0:128] = inv[128:256, 0:128] + t[128:256].T
        diag[128:256, 128:256] = inv[128:256, 128:256] + t[256:384]
        column[:, 0:128] = c[0:32]
        column[:, 128:256] = c[32:64]


def call(kernel, outs, args, scratch=(), scalars=0):
    many = isinstance(outs, list)
    return pl.pallas_call(
        kernel,
        out_shape=outs,
        in_specs=[SMEM] * scalars + [VMEM] * (len(args) - scalars),
        out_specs=[VMEM] * len(outs) if many else VMEM,
        scratch_shapes=list(scratch),
        compiler_params=PARAMS,
    )(*args)


def per_device(
    inverse_pool, factor_one, factor_two, diag_inv_one, diag_inv_two, struct_one, struct_two
):
    row_count, width = factor_one.shape
    f32 = jnp.float32
    core = lax.axis_index("core")
    first = core == 0
    struct = jnp.where(first, struct_one, struct_two)
    mask = lax.dynamic_slice_in_dim(struct, lax.axis_index(("x", "zh")) * 4, 4)
    sibling_pool = lax.ppermute(inverse_pool, "core", SWAP)

    both = jnp.broadcast_to(
        jnp.stack([factor_one, factor_two])[None], (4, 2, row_count, width)
    ).reshape(8, row_count, width)
    rows = exchange(both, ("zl", "core")).reshape(4, 2 * row_count, width)
    rows = rows * mask.astype(jnp.bfloat16)[:, None, None]
    rows = lax.optimization_barrier(rows)
    turned = lax.ppermute(rows, AXES, TURN)
    around = lax.all_gather(rows.reshape(256, width), "y")
    turned, around = lax.optimization_barrier((turned, around))
    strip = gather(turned, "x", 4)

    quarter = jax.ShapeDtypeStruct((256, width), f32)
    diag, *parts = call(
        multiply_kernel,
        [jax.ShapeDtypeStruct((384, 128), f32)] + [quarter] * 4,
        (inverse_pool, sibling_pool, strip, around),
        [pltpu.VMEM((1024, width), jnp.bfloat16), pltpu.VMEM((4, 256, width), f32)],
    )
    shard = jnp.sum(exchange(diag.reshape(16, 24, 128), ("x", "y")), axis=0)
    parts = rotate(parts, "y")
    shard = jnp.sum(gather(shard, ("zh", "zl"), 16), axis=0)
    parts = call(
        turn_kernel,
        [jax.ShapeDtypeStruct((2 * row_count, width), f32)] * 4,
        parts,
        [pltpu.VMEM((256, width), f32)],
    )
    parts = [parts[0]] + [
        lax.ppermute(parts[s], "zl", [(i, i ^ s) for i in range(4)]) for s in (1, 2, 3)
    ]
    half = jax.ShapeDtypeStruct((2 * row_count, 128), f32)
    stay, leave = call(split_kernel, [half, half], (mask, *parts), scalars=1)
    total = gather(shard, ("x", "y"), 16).reshape(384, 128)
    finals = lax.all_gather(jnp.concatenate([total, leave]), "core")
    wide = jax.ShapeDtypeStruct((row_count, width), jnp.bfloat16)
    square = jax.ShapeDtypeStruct((width, width), f32)
    return tuple(
        call(
            finish_kernel,
            [wide, wide, square, square],
            (finals, stay, diag_inv_one, diag_inv_two),
        )
    )


def solution(mesh):
    fine = Mesh(mesh.devices.reshape(SIZES), AXES)
    rows = P(AXES, None)
    in_specs = (P(("x", "zh"), ("zl", "y", "core")), rows, rows, P(), P(), P(), P())
    out_specs = (rows, rows, P(), P())
    return jax.shard_map(
        per_device, mesh=fine, in_specs=in_specs, out_specs=out_specs, check_vma=False
    )
```
